32 devices in a mesh: dom: 8 (over z, y), mp: 4 (over x, core).
Axes of the slice: x: 2, y: 2, z: 4, core: 2. Of those that a mesh axis runs over, the one named last changes fastest.
Arguments:
- grid_feat: bfloat16 [32768, 256], P(('dom', 'mp')), may hold values from -6 to 6
- grid_target: int32 [32768], P(('dom', 'mp')), may hold values from 0 to 8191, as said below
- enc_w1: bfloat16 [256, 512], replicated, may hold values from -0.375 to 0.375
- enc_b1: float32 [512], replicated, may hold values from -3 to 3
- enc_w2: bfloat16 [512, 512], replicated, may hold values from -0.25 to 0.25
- enc_gain: float32 [512], replicated, may hold values from 0.25 to 1.75
- mesh_embed: bfloat16 [8192, 512], P('dom', 'mp'), may hold values from -6 to 6
- nbr_blocks: int32 [128, 16], P('dom'), may hold values from 0 to 127, as said below
- attn_bias: float32 [8, 16, 8192], P('mp', None, 'dom'), may hold values from -2 to 300
- ln_gain: float32 [2, 2, 512], replicated, may hold values from 0.25 to 1.75
- qkv_w: bfloat16 [2, 3, 512, 512], P(None, None, None, 'mp'), may hold values from -0.25 to 0.25
- out_w: bfloat16 [2, 512, 512], P(None, 'mp'), may hold values from -0.25 to 0.25
- up_w: bfloat16 [2, 512, 2048], P(None, None, 'mp'), may hold values from -0.25 to 0.25
- down_w: bfloat16 [2, 2048, 512], P(None, 'mp'), may hold values from -0.125 to 0.125
Outputs:
- mesh_out: bfloat16 [8192, 512], P('dom', 'mp')
The draws below stay inside these ranges and needn't reach their ends.
Inputs may be any that keep to these rules, and one draw needn't show every extreme that they name: `grid_target`: among the 1024 grid nodes of one device (devices in the order dom, then mp), at most 256 have targets among the mesh nodes e * 1024 to (e + 1) * 1024 - 1 of one dom index e, and in every draw some dom index receives exactly 256 from every device. `nbr_blocks`: row b lists 16 different blocks, b itself among them, all within the 24 blocks that start at (b // 16) * 16 - 4, counted around the cycle of 128 blocks.
All inputs are finite; a program needn't handle non-finite values.
Results may differ from the reference program's by a relative error of at most 0.014.
Values may be sent and summed in bfloat16 or wider, within the bound.
A program may use at most 128 MiB of HBM per device.

```python
import jax
import jax.numpy as jnp
from jax import lax

D = 512
HEADS = 8
HEAD_DIM = 64
FF = 2048
F_IN = 256
LAYERS = 2
BLK = 64
NBLK = 16
HB = 4
GR_DEV = 1024
BLOCKS_DEV = 16
CAP = 256
M_DEV = 1024
MESH = 8192
BLOCKS = 128
GRID = 32768
N_DOM = 8


def draw_grid_target(key, part):
    dom_total = MESH // M_DEV
    slot_total = dom_total * CAP
    spread_top = max(1, (1 << 29) // slot_total)
    key_full, key_rows = jax.random.split(jax.random.fold_in(key, 11))
    full_dom = jax.random.randint(key_full, (), 0, dom_total)

    def one_device(device_key):
        key_a, key_b, key_c = jax.random.split(device_key, 3)
        slot_ids = jnp.arange(slot_total, dtype=jnp.int32)
        scores = jax.random.randint(key_a, (slot_total,), 0, spread_top) * slot_total + slot_ids
        scores = jnp.where(slot_ids // CAP == full_dom, (1 << 30) + slot_ids, scores)
        chosen = lax.top_k(scores, GR_DEV)[1]
        chosen = chosen[jax.random.permutation(key_b, GR_DEV)]
        target_node = jax.random.randint(key_c, (GR_DEV,), 0, M_DEV)
        return (chosen // CAP * M_DEV + target_node).astype(jnp.int32)
    device_keys = jax.random.split(key_rows, GRID // GR_DEV)
    return jax.vmap(one_device)(device_keys).reshape(GRID)


def draw_nbr_blocks(key, part):
    window_span = BLOCKS_DEV + 2 * HB
    slot_ids = jnp.arange(window_span, dtype=jnp.int32)

    def one_block(block_id, block_key):
        device_id = block_id // BLOCKS_DEV
        own_slot = block_id - device_id * BLOCKS_DEV + HB
        scores = jax.random.randint(block_key, (window_span,), 0, 1 << 16) * window_span + slot_ids
        scores = jnp.where(slot_ids == own_slot, 1 << 30, scores)
        chosen = lax.top_k(scores, NBLK)[1]
        return ((device_id * BLOCKS_DEV - HB + chosen) % BLOCKS).astype(jnp.int32)
    block_keys = jax.random.split(jax.random.fold_in(key, 7), BLOCKS)
    return jax.vmap(one_block)(jnp.arange(BLOCKS, dtype=jnp.int32), block_keys)


def draw_attn_bias(key, part):
    key_a = jax.random.fold_in(jax.random.fold_in(key, 5), 0)
    base_bias = jax.random.uniform(key_a, (HEADS, NBLK, MESH), jnp.float32, -2.0, 2.0)
    return base_bias


def steps_of(stream_key, extent, pieces, smallest, high):
    def one(position, shards_of):
        draws = jax.random.uniform(jax.random.fold_in(jax.random.fold_in(stream_key, 6), position), (shards_of,), jnp.float32, smallest / len(pieces), high / len(pieces))
        return jnp.repeat(jnp.exp(draws), extent[position] // shards_of).reshape((-1,) + (1,) * (len(extent) - position - 1))

    gain = one(*pieces[0])
    for cut in pieces[1:]:
        gain = gain * one(*cut)
    return gain


def normal_values(rng, extent, scale, most, cuts=(), kind=jnp.bfloat16):
    factor_of = steps_of(rng, extent, cuts, -0.22, 0.18) if cuts else 1.0
    drawn = jax.random.normal(rng, extent, jnp.float32) * scale * factor_of
    return jnp.minimum(jnp.maximum(drawn, -most), most).astype(kind)


def setup_inputs(seed: int = 0) -> dict:
    key_of = jax.random.split(jax.random.key(seed), 15)
    return {
        "grid_feat": normal_values(key_of[0], (GRID, F_IN), 1.0, 6.0, ((0, 32),)),
        "grid_target": draw_grid_target(jax.random.fold_in(key_of[14], 71), 0),
        "enc_w1": normal_values(key_of[2], (F_IN, D), F_IN ** -0.5, 0.375),
        "enc_b1": normal_values(key_of[3], (D,), 0.5, 3.0, (), jnp.float32),
        "enc_w2": normal_values(key_of[4], (D, D), D ** -0.5, 0.25),
        "enc_gain": jnp.clip(1.0 + 0.15 * jax.random.normal(key_of[5], (D,), jnp.float32), 0.25, 1.75),
        "mesh_embed": normal_values(key_of[6], (MESH, D), 1.0, 6.0, ((0, 8), (1, 4))),
        "nbr_blocks": draw_nbr_blocks(jax.random.fold_in(key_of[14], 71), 0),
        "attn_bias": draw_attn_bias(jax.random.fold_in(key_of[14], 71), 0),
        "ln_gain": jnp.clip(1.0 + 0.15 * jax.random.normal(key_of[9], (LAYERS, 2, D), jnp.float32), 0.25, 1.75),
        "qkv_w": normal_values(key_of[10], (LAYERS, 3, D, D), D ** -0.5, 0.25, ((3, 4),)),
        "out_w": normal_values(key_of[11], (LAYERS, D, D), D ** -0.5, 0.25, ((1, 4),)),
        "up_w": normal_values(key_of[12], (LAYERS, D, FF), D ** -0.5, 0.25, ((2, 4),)),
        "down_w": normal_values(key_of[13], (LAYERS, FF, D), FF ** -0.5, 0.125, ((1, 4),)),
    }


EPS = 1e-05

def normalize(values, gain_vector):
    values = values.astype(jnp.float32)
    row_mean = lax.optimization_barrier(jnp.mean(values, axis=-1, keepdims=True))
    centered = values - row_mean
    variance = lax.optimization_barrier(jnp.mean(centered * centered, axis=-1, keepdims=True))
    return centered * lax.rsqrt(variance + EPS) * gain_vector

def encode(features, enc_w1, enc_b1, enc_w2, enc_gain):
    first = jnp.dot(features, enc_w1, preferred_element_type=jnp.float32) + enc_b1
    first = jax.nn.silu(first).astype(jnp.bfloat16)
    second = jnp.dot(first, enc_w2, preferred_element_type=jnp.float32)
    return normalize(second, enc_gain).astype(jnp.bfloat16)

def attend(queries, key_rows, value_rows, nbr_blocks, attn_bias):
    query_blocks = queries.reshape(N_DOM, BLOCKS_DEV, BLK, HEADS, HEAD_DIM)
    key_blocks = key_rows.reshape(BLOCKS, BLK, HEADS, HEAD_DIM)
    value_blocks = value_rows.reshape(BLOCKS, BLK, HEADS, HEAD_DIM)
    block_lists = nbr_blocks.reshape(N_DOM, BLOCKS_DEV, NBLK)
    bias_rows = jnp.transpose(attn_bias.reshape(HEADS, NBLK, N_DOM, BLOCKS_DEV, BLK), (2, 3, 0, 4, 1))

    def one_group(block_item):
        group_query, group_lists, group_bias = block_item
        group_keys = key_blocks[group_lists].reshape(BLOCKS_DEV, NBLK * BLK, HEADS, HEAD_DIM).astype(jnp.float32)
        group_values = value_blocks[group_lists].reshape(BLOCKS_DEV, NBLK * BLK, HEADS, HEAD_DIM).astype(jnp.float32)
        scores = jnp.einsum('tqhe,tkhe->thqk', group_query.astype(jnp.float32), group_keys) * HEAD_DIM ** (-0.5)
        scores = scores.reshape(BLOCKS_DEV, HEADS, BLK, NBLK, BLK) + group_bias[..., None]
        row_max = lax.optimization_barrier(jnp.max(scores, axis=(3, 4), keepdims=True))
        exponent = jnp.exp(scores - row_max)
        weights = (exponent / lax.optimization_barrier(jnp.sum(exponent, axis=(3, 4), keepdims=True))).astype(jnp.bfloat16)
        weights = weights.reshape(BLOCKS_DEV, HEADS, BLK, NBLK * BLK).astype(jnp.float32)
        attended = jnp.einsum('thqk,tkhe->tqhe', weights, group_values)
        return attended.astype(jnp.bfloat16).reshape(BLOCKS_DEV * BLK, HEADS * HEAD_DIM)
    return lax.map(one_group, (query_blocks, block_lists, bias_rows)).reshape(MESH, D)

def reference(grid_feat, grid_target, enc_w1, enc_b1, enc_w2, enc_gain, mesh_embed, nbr_blocks, attn_bias, ln_gain, qkv_w, out_w, up_w, down_w):
    features = grid_feat.reshape(GRID // GR_DEV, GR_DEV, F_IN)
    targets = grid_target.reshape(GRID // GR_DEV, GR_DEV)

    def add_block(running, block_item):
        message = encode(block_item[0], enc_w1, enc_b1, enc_w2, enc_gain)
        return (running.at[block_item[1]].add(message.astype(jnp.float32)), None)
    gathered, _ = lax.scan(add_block, jnp.zeros((MESH, D), jnp.float32), (features, targets))
    stream = (mesh_embed.astype(jnp.float32) + gathered).astype(jnp.bfloat16)
    for layer_index in range(LAYERS):
        normed = normalize(stream, ln_gain[layer_index, 0]).astype(jnp.bfloat16)
        queries = jnp.dot(normed, qkv_w[layer_index, 0], preferred_element_type=jnp.float32).astype(jnp.bfloat16)
        key_rows = jnp.dot(normed, qkv_w[layer_index, 1], preferred_element_type=jnp.float32).astype(jnp.bfloat16)
        value_rows = jnp.dot(normed, qkv_w[layer_index, 2], preferred_element_type=jnp.float32).astype(jnp.bfloat16)
        attended = attend(queries, key_rows, value_rows, nbr_blocks, attn_bias)
        stream = (stream.astype(jnp.float32) + jnp.dot(attended, out_w[layer_index], preferred_element_type=jnp.float32)).astype(jnp.bfloat16)
        normed = normalize(stream, ln_gain[layer_index, 1]).astype(jnp.bfloat16)
        hidden = jax.nn.silu(jnp.dot(normed, up_w[layer_index], preferred_element_type=jnp.float32)).astype(jnp.bfloat16)
        stream = (stream.astype(jnp.float32) + jnp.dot(hidden, down_w[layer_index], preferred_element_type=jnp.float32)).astype(jnp.bfloat16)
    return stream
```

```python
import functools

import jax
import jax.numpy as jnp
from jax import lax
from jax.experimental import pallas as pl
from jax.experimental.pallas import tpu as pltpu
from jax.sharding import PartitionSpec as P

HEAD_DIM = 64
BLK = 64
NBLK = 16
HB = 4
EPS = 1e-05
LOG2E = 1.4426950408889634
F32 = jnp.float32
BF16 = jnp.bfloat16
MESH = pl.DeviceIdType.MESH


def normalize(values, gain_row):
    row_mean = jnp.mean(values, axis=-1, keepdims=True)
    centered = values - row_mean
    variance = jnp.mean(centered * centered, axis=-1, keepdims=True)
    return centered * lax.rsqrt(variance + EPS) * gain_row


def silu(v):
    return v / (1.0 + jnp.exp(-v))


def mm(a, b):
    return jnp.dot(a, b, preferred_element_type=F32)


def mega(
    n_dom,
    n_mp,
    layers,
    nbr,
    feat,
    target,
    w1,
    b1,
    w2,
    egain,
    embed,
    bias_in,
    ln_gain,
    qkv_hbm,
    out_hbm,
    up_hbm,
    down_hbm,
    result,
    bias,
    qkv_w,
    sbuf,
    sland,
    rbuf,
    rland,
    acc,
    psend,
    precv,
    xrow,
    nrm,
    kv0,
    kv1,
    qs,
    att,
    arecv,
    gout,
    gup,
    gdown,
    d_send,
    d_recv,
    p_send,
    p_recv,
    ag_send,
    ag_recv,
    w_send,
    w_recv,
    h_send,
    h_recv,
    a_send,
    a_recv,
    f_send,
    f_recv,
    l_sem,
):
    dom = lax.axis_index("dom")
    m = lax.axis_index("mp")
    rows = feat.shape[0]
    cap = sbuf.shape[1]
    nodes = embed.shape[0]
    cols = embed.shape[1]
    quarter = nodes // n_mp
    qblk = quarter // BLK
    heads = cols // HEAD_DIM
    local_blocks = nodes // BLK
    peers = [m + 1 - 2 * (m % 2), (m + 2) % 4, 3 - m]

    def dev(d, p):
        return (d, p)

    barrier = pltpu.get_barrier_semaphore()
    for k in range(1, n_dom):
        pl.semaphore_signal(barrier, inc=1, device_id=dev((dom + k) % n_dom, m), device_id_type=MESH)
    for p in peers:
        pl.semaphore_signal(barrier, inc=1, device_id=dev(dom, p), device_id_type=MESH)

    owner = target[...] // nodes
    node = target[...] % nodes
    row_e = lax.broadcasted_iota(jnp.int32, (n_dom, rows), 0)
    member = (row_e == owner).astype(F32)
    before = (
        lax.broadcasted_iota(jnp.int32, (rows, rows), 0)
        < lax.broadcasted_iota(jnp.int32, (rows, rows), 1)
    ).astype(F32).astype(BF16)
    count = mm(member.astype(BF16), before)
    rank = jnp.sum(count * member, axis=0, keepdims=True).astype(jnp.int32)
    slot = owner * cap + rank
    hi = (node // 32).astype(F32)
    lo = (node % 32).astype(F32)
    pick = lax.broadcasted_iota(jnp.int32, (16, rows), 0)
    parts = jnp.where(
        pick == 0, hi, jnp.where(pick == 1, lo, jnp.where(pick == 2, 1.0, 0.0))
    ).astype(BF16)
    features = feat[...]

    def outgoing(k):
        e = (dom + k) % n_dom
        here = (
            lax.broadcasted_iota(jnp.int32, (cap, rows), 0) == slot - e * cap
        ).astype(F32).astype(BF16)
        sbuf[k] = mm(here, features).astype(BF16)
        where_to = lax.dot_general(parts, here, (((1,), (1,)), ((), ())), preferred_element_type=F32)
        landed = where_to[0:1] * 32.0 + where_to[1:2]
        landed = jnp.where(where_to[2:3] > 0.5, landed, -1.0).astype(jnp.int32)
        sland[k] = jnp.broadcast_to(landed, (8, cap))

    def d_copies(k):
        target_dev = dev((dom + k) % n_dom, m)
        return (
            pltpu.make_async_remote_copy(
                sbuf.at[k], rbuf.at[k], d_send.at[0, k], d_recv.at[0, k],
                device_id=target_dev, device_id_type=MESH,
            ),
            pltpu.make_async_remote_copy(
                sland.at[k], rland.at[k], d_send.at[1, k], d_recv.at[1, k],
                device_id=target_dev, device_id_type=MESH,
            ),
        )

    order = sorted(range(1, n_dom), key=lambda k: -min(k, n_dom - k))
    outgoing(order[0])
    pl.semaphore_wait(barrier, n_dom - 1 + len(peers))
    started = {}

    weights = ((out_hbm, gout), (up_hbm, gup), (down_hbm, gdown))
    local = [pltpu.make_async_copy(qkv_hbm, qkv_w, l_sem.at[layers, 0])]
    for layer in range(layers):
        for i, (own, got) in enumerate(weights):
            local.append(
                pltpu.make_async_copy(own.at[layer], got.at[layer, 3], l_sem.at[layer, i])
            )

    def w_copies(layer, hop):
        out = []
        for i, (own, got) in enumerate(weights):
            if hop < 2:
                src = own.at[layer]
                p = peers[hop]
            else:
                src = got.at[layer, 1]
                p = peers[0]
            out.append(
                pltpu.make_async_remote_copy(
                    src, got.at[layer, hop], w_send.at[layer, hop, i], w_recv.at[layer, hop, i],
                    device_id=dev(dom, p), device_id_type=MESH,
                )
            )
        return out

    wc = {(l, h): w_copies(l, h) for l in range(layers) for h in range(3)}

    def start_all(copies):
        for c in copies:
            c.start()

    for n, k in enumerate(order):
        if n:
            outgoing(k)
        started[k] = d_copies(k)
        start_all(started[k])
    start_all(wc[0, 1])
    start_all(wc[0, 0])
    start_all(local)
    outgoing(0)
    for b in range(local_blocks):
        bias[b] = jnp.concatenate(
            [bias_in[h, :, b * BLK : (b + 1) * BLK] for h in range(heads)], axis=1
        ) * LOG2E

    def consume(buf, land, first):
        v = mm(buf, w1[...]) + b1[...]
        message = normalize(mm(silu(v).astype(BF16), w2[...]), egain[...]).astype(BF16)
        scatter = (
            lax.broadcasted_iota(jnp.int32, (nodes, cap), 0) == land[0:1]
        ).astype(F32).astype(BF16)
        if first:
            acc[...] = mm(scatter, message)
        else:
            acc[...] += mm(scatter, message)

    consume(sbuf[0], sland[0], True)
    mine = pl.ds(pl.multiple_of(m * cols, cols), cols)
    acc[:, mine] += embed[...].astype(F32)
    for k in order:
        for c in started[k]:
            c.wait_recv()
        consume(rbuf[k], rland[k], False)

    def rows_of(p):
        return pl.ds(pl.multiple_of(p * quarter, quarter), quarter)

    def p_copy(i, p):
        return pltpu.make_async_remote_copy(
            psend.at[i], precv.at[i], p_send.at[i], p_recv.at[i],
            device_id=dev(dom, p), device_id_type=MESH,
        )

    pc = [p_copy(0, peers[0]), p_copy(1, peers[0]), p_copy(2, peers[1])]
    psend[0] = acc[rows_of(peers[2]), :].astype(BF16)
    pc[0].start()
    psend[1] = acc[rows_of(peers[0]), :].astype(BF16)
    pc[1].start()
    pc[0].wait_recv()
    psend[2] = (acc[rows_of(peers[1]), :] + precv[0].astype(F32)).astype(BF16)
    pc[2].start()
    pc[1].wait_recv()
    total = acc[rows_of(m), :] + precv[1].astype(F32)
    for c in wc[0, 1]:
        c.wait_recv()
    start_all(wc[0, 2])
    for c in local:
        c.wait()
    pc[2].wait_recv()
    total = total + precv[2].astype(F32)
    xrow[...] = total.astype(BF16)

    lane = lax.broadcasted_iota(jnp.int32, (BLK, cols), 1) // HEAD_DIM
    ones = jnp.ones((NBLK * BLK, cols), BF16)
    block_count = local_blocks * n_dom

    def slot_of(b, t):
        away = nbr[b, t] - (dom * local_blocks - HB)
        away = jnp.where(away < 0, away + block_count, away)
        away = jnp.where(away >= block_count, away - block_count, away)
        return jnp.minimum(away, local_blocks + 2 * HB - 1)

    pending = []
    for layer in range(layers):
        kv = (kv0, kv1)[layer]
        nrm[layer, 3] = normalize(xrow[...].astype(F32), ln_gain[layer, 0:1, :]).astype(BF16)
        half = quarter // 2

        def ag_copy(i, src, dst, part, p):
            return pltpu.make_async_remote_copy(
                nrm.at[layer, src, part], nrm.at[layer, dst, part],
                ag_send.at[layer, i], ag_recv.at[layer, i],
                device_id=dev(dom, p), device_id_type=MESH,
            )

        halves = [pl.ds(0, half), pl.ds(half, half)]
        ag = [ag_copy(1 + i, 3, 1, halves[i], peers[1]) for i in range(2)]
        ag.append(ag_copy(0, 3, 0, pl.ds(0, quarter), peers[0]))
        relay = [ag_copy(3 + i, 1, 2, halves[i], peers[0]) for i in range(2)]
        start_all(ag)
        halo = [
            pltpu.make_async_remote_copy(
                kv.at[pl.ds(HB, HB)], kv.at[pl.ds(HB + local_blocks, HB)],
                h_send.at[layer, 0], h_recv.at[layer, 0],
                device_id=dev((dom + n_dom - 1) % n_dom, m), device_id_type=MESH,
            ),
            pltpu.make_async_remote_copy(
                kv.at[pl.ds(local_blocks, HB)], kv.at[pl.ds(0, HB)],
                h_send.at[layer, 1], h_recv.at[layer, 1],
                device_id=dev((dom + 1) % n_dom, m), device_id_type=MESH,
            ),
        ]

        def project(r, p):
            block = nrm[layer, r]
            spot = pl.ds(HB + p * qblk, qblk)
            kv[spot, :, 0:cols] = mm(block, qkv_w[layer, 1]).astype(BF16).reshape(qblk, BLK, cols)
            kv[spot, :, cols : 2 * cols] = (
                mm(block, qkv_w[layer, 2]).astype(BF16).reshape(qblk, BLK, cols)
            )

            @pl.when(p == 0)
            def _():
                halo[0].start()

            @pl.when(p == n_mp - 1)
            def _():
                halo[1].start()

        def project_q(r, p):
            q = mm(nrm[layer, r], qkv_w[layer, 0]) * (HEAD_DIM ** (-0.5) * LOG2E)
            qs[layer, rows_of(p), :] = q.astype(BF16)

        project(3, m)
        ag[2].wait_recv()
        project(0, peers[0])
        for i in range(2):
            ag[i].wait_recv()
            relay[i].start()
        project(1, peers[1])
        for c in relay:
            c.wait_recv()
        project(2, peers[2])
        if layer + 1 < layers:
            start_all(wc[layer + 1, 1][0:2])
            start_all(wc[layer + 1, 0][0:2])
        if layer > 0:
            for c in wc[layer, 1][0:2]:
                c.wait_recv()
            start_all(wc[layer, 2][0:2])
        project_q(3, m)
        for r in range(3):
            project_q(r, peers[r])
        for c in halo:
            c.wait_recv()

        def attend(p):
            for i in range(qblk):
                b = p * qblk + i
                span = pl.ds(pl.multiple_of(b * BLK, BLK), BLK)
                q = qs[layer, span, :]
                qbd = jnp.concatenate(
                    [jnp.where(lane == h, q.astype(F32), 0.0) for h in range(heads)], axis=0
                ).astype(BF16)
                picked = [kv[slot_of(b, t)] for t in range(NBLK)]
                keys = jnp.concatenate([x[:, 0:cols] for x in picked], axis=0)
                values = jnp.concatenate(
                    [jnp.concatenate([x[:, cols : 2 * cols] for x in picked], axis=0), ones], axis=1
                )
                s = lax.dot_general(keys, qbd, (((1,), (1,)), ((), ())), preferred_element_type=F32)
                s = s.reshape(NBLK, BLK, heads * BLK) + bias[b][:, None, :]
                s = s.reshape(NBLK * BLK, heads * BLK)
                e = jnp.exp2(s - jnp.max(s, axis=0, keepdims=True)).astype(BF16)
                o = lax.dot_general(e, values, (((0,), (0,)), ((), ())), preferred_element_type=F32)
                o = o[:, 0:cols] / o[:, cols : 2 * cols]
                merged = o[0:BLK]
                for h in range(1, heads):
                    merged = jnp.where(lane == h, o[h * BLK : (h + 1) * BLK], merged)
                att[layer, span, :] = merged.astype(BF16)

        ac = []
        for r in (2, 1, 0):
            attend(peers[r])
            c = pltpu.make_async_remote_copy(
                att.at[layer, rows_of(peers[r])], arecv.at[layer, r],
                a_send.at[layer, r], a_recv.at[layer, r],
                device_id=dev(dom, peers[r]), device_id_type=MESH,
            )
            c.start()
            ac.append(c)
        if layer > 0:
            for c in wc[layer, 1][2:3]:
                c.wait_recv()
            start_all(wc[layer, 2][2:3])
        attend(m)
        for c in wc[layer, 0] + wc[layer, 2]:
            c.wait_recv()
        y = xrow[...].astype(F32) + mm(att[layer, rows_of(m), :], gout[layer, 3])
        for c in ac:
            c.wait_recv()
        for r in range(3):
            y = y + mm(arecv[layer, r], gout[layer, r])
        if layer + 1 < layers:
            start_all(wc[layer + 1, 1][2:3])
            start_all(wc[layer + 1, 0][2:3])
        x1 = y.astype(BF16).astype(F32)
        n2 = normalize(x1, ln_gain[layer, 1:2, :]).astype(BF16)
        total = x1
        for r in (3, 0, 1, 2):
            total = total + mm(silu(mm(n2, gup[layer, r])).astype(BF16), gdown[layer, r])
        xrow[...] = total.astype(BF16)
        pending += ag + relay + halo + ac

    fc = []
    for r in range(3):
        c = pltpu.make_async_remote_copy(
            xrow.at[:, pl.ds(pl.multiple_of(peers[r] * cols, cols), cols)],
            result.at[rows_of(m), :],
            f_send.at[r], f_recv.at[r],
            device_id=dev(dom, peers[r]), device_id_type=MESH,
        )
        c.start()
        fc.append(c)
    result[rows_of(m), :] = xrow[:, mine]
    for k in order:
        for c in started[k]:
            c.wait_send()
    for c in pc + pending:
        c.wait_send()
    for key in wc:
        for c in wc[key]:
            c.wait_send()
    for c in fc:
        c.wait()


def shards(
    grid_feat,
    grid_target,
    enc_w1,
    enc_b1,
    enc_w2,
    enc_gain,
    mesh_embed,
    nbr_blocks,
    attn_bias,
    ln_gain,
    qkv_w,
    out_w,
    up_w,
    down_w,
):
    n_dom = lax.axis_size("dom")
    n_mp = lax.axis_size("mp")
    rows, f_in = grid_feat.shape
    width = enc_w2.shape[1]
    cols = width // n_mp
    nodes = mesh_embed.shape[0]
    local_blocks = nodes // BLK
    heads = cols // HEAD_DIM
    layers = ln_gain.shape[0]
    cap = 2 * rows // n_dom
    quarter = nodes // n_mp
    ff = up_w.shape[2]
    vmem = pl.BlockSpec(memory_space=pltpu.VMEM)
    dma = pltpu.SemaphoreType.DMA
    window = local_blocks + 2 * HB
    return pl.pallas_call(
        functools.partial(mega, n_dom, n_mp, layers),
        out_shape=jax.ShapeDtypeStruct((nodes, cols), BF16),
        in_specs=[pl.BlockSpec(memory_space=pltpu.SMEM)] + [vmem] * 9 + [pl.BlockSpec(memory_space=pl.ANY)] * 4,
        out_specs=vmem,
        scratch_shapes=[
            pltpu.VMEM((local_blocks, NBLK, heads * BLK), F32),
            pltpu.VMEM(qkv_w.shape, BF16),
            pltpu.VMEM((n_dom, cap, f_in), BF16),
            pltpu.VMEM((n_dom, 8, cap), jnp.int32),
            pltpu.VMEM((n_dom, cap, f_in), BF16),
            pltpu.VMEM((n_dom, 8, cap), jnp.int32),
            pltpu.VMEM((nodes, width), F32),
            pltpu.VMEM((3, quarter, width), BF16),
            pltpu.VMEM((3, quarter, width), BF16),
            pltpu.VMEM((quarter, width), BF16),
            pltpu.VMEM((layers, 4, quarter, width), BF16),
            pltpu.VMEM((window, BLK, 2 * cols), BF16),
            pltpu.VMEM((window, BLK, 2 * cols), BF16),
            pltpu.VMEM((layers, nodes, cols), BF16),
            pltpu.VMEM((layers, nodes, cols), BF16),
            pltpu.VMEM((layers, 3, quarter, cols), BF16),
            pltpu.VMEM((layers, 4, cols, width), BF16),
            pltpu.VMEM((layers, 4, width, ff), BF16),
            pltpu.VMEM((layers, 4, ff, width), BF16),
            dma((2, n_dom)),
            dma((2, n_dom)),
            dma((3,)),
            dma((3,)),
            dma((layers, 5)),
            dma((layers, 5)),
            dma((layers, 3, 3)),
            dma((layers, 3, 3)),
            dma((layers, 2)),
            dma((layers, 2)),
            dma((layers, 3)),
            dma((layers, 3)),
            dma((3,)),
            dma((3,)),
            dma((layers + 1, 3)),
        ],
        compiler_params=pltpu.CompilerParams(
            collective_id=0, has_side_effects=True, vmem_limit_bytes=60 * 1024 * 1024
        ),
    )(
        nbr_blocks,
        grid_feat,
        grid_target.reshape(1, rows),
        enc_w1,
        enc_b1.reshape(1, width),
        enc_w2,
        enc_gain.reshape(1, width),
        mesh_embed,
        attn_bias,
        ln_gain,
        qkv_w,
        out_w,
        up_w,
        down_w,
    )


def solution(mesh):
    placed = (
        P(("dom", "mp"), None),
        P(("dom", "mp")),
        P(),
        P(),
        P(),
        P(),
        P("dom", "mp"),
        P("dom", None),
        P("mp", None, "dom"),
        P(),
        P(None, None, None, "mp"),
        P(None, "mp", None),
        P(None, None, "mp"),
        P(None, "mp", None),
    )
    return jax.shard_map(
        shards, mesh=mesh, in_specs=placed, out_specs=P("dom", "mp"), check_vma=False
    )
```

```python
import functools

import jax
import jax.numpy as jnp
from jax import lax
from jax.experimental import pallas as pl
from jax.experimental.pallas import tpu as pltpu
from jax.sharding import PartitionSpec as P

HEAD_DIM = 64
BLK = 64
NBLK = 16
HB = 4
EPS = 1e-05
LOG2E = 1.4426950408889634
F32 = jnp.float32
BF16 = jnp.bfloat16
MESH = pl.DeviceIdType.MESH


def normalize(values, gain_row):
    row_mean = jnp.mean(values, axis=-1, keepdims=True)
    centered = values - row_mean
    variance = jnp.mean(centered * centered, axis=-1, keepdims=True)
    return centered * lax.rsqrt(variance + EPS) * gain_row


def silu(v):
    return v / (1.0 + jnp.exp(-v))


def mm(a, b):
    return jnp.dot(a, b, preferred_element_type=F32)


def dot_nt(a, b):
    return lax.dot_general(a, b, (((1,), (1,)), ((), ())), preferred_element_type=F32)


def dot_tn(a, b):
    return lax.dot_general(a, b, (((0,), (0,)), ((), ())), preferred_element_type=F32)


def remote(src, dst, send, recv, where):
    return pltpu.make_async_remote_copy(
        src, dst, send, recv, device_id=where, device_id_type=MESH
    )


def mega(
    n_dom,
    n_mp,
    layers,
    nbr,
    feat,
    target,
    w1,
    b1,
    w2,
    egain,
    embed,
    bias_in,
    ln_gain,
    qkv_hbm,
    out_hbm,
    up_hbm,
    down_hbm,
    result,
    bias,
    brecv,
    sbuf,
    sland,
    rbuf,
    rland,
    acc,
    psend,
    precv,
    xsend,
    xrecv,
    xown,
    nown,
    nhalo,
    kbuf,
    vbuf,
    qs,
    att,
    gq,
    gout,
    gup,
    gdown,
    fin,
    d_send,
    d_recv,
    b_send,
    b_recv,
    p_send,
    p_recv,
    x_send,
    x_recv,
    n_send,
    n_recv,
    c_send,
    c_recv,
    h_send,
    h_recv,
    r_send,
    r_recv,
    w_send,
    w_recv,
    f_send,
    f_recv,
    l_sem,
):
    dom = lax.axis_index("dom")
    m = lax.axis_index("mp")
    rows = feat.shape[0]
    cap = sbuf.shape[1]
    nodes, width = acc.shape
    cols = embed.shape[1]
    heads = cols // HEAD_DIM
    local_blocks = nodes // BLK
    per = local_blocks // n_mp
    edge = HB // n_mp
    span = per + 2 * edge
    prow = per // 2 * BLK
    core, side = m % 2, m // 2
    order_of = list(range(edge)) + list(range(per - edge, per)) + list(range(edge, per - edge))
    mine = (dom, m)
    peers = [(dom, m + 1 - 2 * (m % 2)), (dom, (m + 2) % 4), (dom, 3 - m)]
    twin = (dom + 1 - 2 * (dom % 2), m)
    beside = [((dom + n_dom - 1) % n_dom, m), ((dom + 1) % n_dom, m)]

    def across(n):
        e = 0
        bit = 1
        while bit < n_dom:
            own = (dom // bit) % 2
            e = e + ((1 - own) if n & bit else own) * bit
            bit *= 2
        return e

    barrier = pltpu.get_barrier_semaphore()
    for n in range(1, n_dom):
        pl.semaphore_signal(barrier, inc=1, device_id=(across(n), m), device_id_type=MESH)
    for p in peers:
        pl.semaphore_signal(barrier, inc=1, device_id=p, device_id_type=MESH)

    owner = target[...] // nodes
    node = target[...] % nodes
    block = node // BLK
    held_by = block % n_mp
    nth = block // n_mp
    nth = jnp.where(
        nth < edge, nth, jnp.where(nth >= per - edge, nth - (per - 2 * edge), nth + edge)
    )
    place = (((held_by % 2) * 2 + held_by // 2) * per + nth) * BLK + node % BLK
    member = (lax.broadcasted_iota(jnp.int32, (n_dom, rows), 0) == owner).astype(F32)
    lanes = 128
    chunks = rows // lanes
    stacked = jnp.concatenate(
        [member[:, j * lanes : (j + 1) * lanes] for j in range(chunks)], axis=0
    ).astype(BF16)
    row_i = lax.broadcasted_iota(jnp.int32, (lanes, 2 * lanes), 0)
    col_i = lax.broadcasted_iota(jnp.int32, (lanes, 2 * lanes), 1)
    before = ((row_i < col_i) | (col_i >= lanes)).astype(F32).astype(BF16)
    counts = mm(stacked, before)
    running = jnp.zeros((n_dom, lanes), F32)
    ranks = []
    for j in range(chunks):
        part = counts[j * n_dom : (j + 1) * n_dom]
        here = (part[:, 0:lanes] + running) * member[:, j * lanes : (j + 1) * lanes]
        ranks.append(jnp.sum(here, axis=0, keepdims=True))
        running = running + part[:, lanes:]
    rank = jnp.concatenate(ranks, axis=1)
    hi = (place // 32).astype(F32)
    lo = (place % 32).astype(F32)
    pick = lax.broadcasted_iota(jnp.int32, (16, rows), 0)
    parts = jnp.where(
        pick == 0, hi, jnp.where(pick == 1, lo, jnp.where(pick == 2, 1.0, 0.0))
    ).astype(BF16)
    features = feat[...]
    seat = lax.broadcasted_iota(jnp.int32, (cap, rows), 0).astype(F32).astype(BF16)

    def outgoing(n):
        wanted = jnp.where(owner == across(n), rank, -1.0).astype(BF16)
        here = jnp.where(seat == wanted, jnp.ones((), BF16), jnp.zeros((), BF16))
        sbuf[n] = mm(here, features).astype(BF16)
        where_to = dot_nt(parts, here)
        landed = where_to[0:1] * 32.0 + where_to[1:2]
        sland[n] = jnp.where(where_to[2:3] > 0.5, landed, -1.0).astype(jnp.int32)

    def d_copies(n):
        there = (across(n), m)
        return [
            remote(sbuf.at[n], rbuf.at[n], d_send.at[0, n], d_recv.at[0, n], there),
            remote(sland.at[n], rland.at[n], d_send.at[1, n], d_recv.at[1, n], there),
        ]

    def start_all(copies):
        for c in copies:
            c.start()

    sent = []

    def send(c):
        c.start()
        sent.append(c)
        return c

    arrays = ((qkv_hbm, gq), (out_hbm, gout), (up_hbm, gup), (down_hbm, gdown))
    half = dom % 2

    def part_of(ref, lead, i, h):
        size = ref.shape[-2] // 2
        at = pl.ds(pl.multiple_of(h * size, size), size)
        return ref.at[lead + ((slice(None), at) if i == 0 else (at,))]

    def w_copy(k, l, i):
        own, got = arrays[i]
        sems = (w_send.at[k, l, i], w_recv.at[k, l, i])
        if k == 0:
            return remote(part_of(own, (l,), i, half), part_of(got, (l, 2), i, half), *sems, peers[1])
        if k == 1:
            return remote(part_of(got, (l, 2), i, half), part_of(got, (l, 2), i, half), *sems, twin)
        if k == 2:
            return remote(own.at[l], got.at[l, 1], *sems, peers[0])
        h = half if k == 3 else 1 - half
        return remote(part_of(got, (l, 2), i, h), part_of(got, (l, 3), i, h), *sems, peers[0])

    wc = {}

    def w_start(k, l, ids):
        if l < layers:
            for i in ids:
                wc[k, l, i] = send(w_copy(k, l, i))

    def w_wait(k, l, ids):
        if l < layers:
            for i in ids:
                wc[k, l, i].wait_recv()

    def w_forward(l, ids):
        w_wait(0, l, ids)
        w_start(1, l, ids)
        w_start(3, l, ids)

    def w_relay(l, ids):
        w_wait(1, l, ids)
        w_start(4, l, ids)

    def w_ready(l, ids):
        for i in ids:
            local[l, i].wait()
            for k in (2, 3, 4):
                wc[k, l, i].wait_recv()

    local = {
        (l, i): pltpu.make_async_copy(own.at[l], got.at[l, 0], l_sem.at[l, i])
        for l in range(layers)
        for i, (own, got) in enumerate(arrays)
    }

    far = list(range(n_dom - 1, 0, -1))
    outgoing(far[0])
    pl.semaphore_wait(barrier, n_dom - 1 + len(peers))
    moving = {}
    for j, n in enumerate(far):
        if j:
            outgoing(n)
        moving[n] = d_copies(n)
        start_all(moving[n])
        if j == 0:
            w_start(0, 0, (0,))
    w_start(0, 0, (1, 2, 3))
    for l in range(layers):
        w_start(2, l, (0, 1, 2, 3))
    for key in local:
        local[key].start()
    for o in range(n_mp):
        for r, i in enumerate(order_of):
            b = i * n_mp + o
            bias[o, r] = LOG2E * jnp.concatenate(
                [bias_in[h, :, b * BLK : (b + 1) * BLK] for h in range(heads)], axis=1
            )
    bc = [
        send(remote(bias.at[peers[k][1]], brecv.at[k], b_send.at[k], b_recv.at[k], peers[k]))
        for k in range(3)
    ]
    outgoing(0)

    def consume(buf, land, first):
        v = mm(buf, w1[...]) + b1[...]
        message = normalize(mm(silu(v).astype(BF16), w2[...]), egain[...]).astype(BF16)
        step = cap
        spot = lax.broadcasted_iota(jnp.int32, (step, cap), 0).astype(F32).astype(BF16)
        for c in range(nodes // step):
            goal = (land - c * step).astype(F32).astype(BF16)
            scatter = jnp.where(spot == goal, jnp.ones((), BF16), jnp.zeros((), BF16))
            at = slice(c * step, (c + 1) * step)
            if first:
                acc[at] = mm(scatter, message)
            else:
                acc[at] += mm(scatter, message)

    consume(sbuf[0], sland[0], True)
    my_cols = pl.ds(pl.multiple_of(m * cols, cols), cols)
    for o in range(n_mp):
        for r, i in enumerate(order_of):
            b = i * n_mp + o
            at = (((o % 2) * 2 + o // 2) * per + r) * BLK
            acc[at : at + BLK, my_cols] += embed[b * BLK : (b + 1) * BLK].astype(F32)
    w_forward(0, (0,))
    w_start(0, 1, (0,))
    near = list(range(1, n_dom // 2))
    late = list(range(n_dom - 1, n_dom // 2 - 1, -1))
    for j, n in enumerate(near + late):
        for c in moving[n]:
            c.wait_recv()
        consume(rbuf[n], rland[n], False)
        if j == 0:
            w_relay(0, (0,))
        if j == len(near) - 1:
            w_forward(0, (1, 2, 3))
            w_start(0, 1, (1, 2))
        if j == len(near) + len(late) // 2 - 1:
            w_forward(1, (0,))

    def acc_rows(c, rel, part):
        at = (c * 2 + (side + rel) % 2) * per * BLK + part * prow
        return pl.ds(pl.multiple_of(at, BLK), prow)

    pieces = [(0, 0), (1, 0), (0, 1), (1, 1)]
    pc = {}
    for rel, part in pieces:
        psend[rel, part] = acc[acc_rows(1 - core, rel, part), :].astype(BF16)
        pc[rel, part] = send(
            remote(psend.at[rel, part], precv.at[rel, part], p_send.at[rel, part], p_recv.at[rel, part], peers[0])
        )
    xc = {}
    for rel, part in pieces:
        pc[rel, part].wait_recv()
        xsend[rel, part] = (
            acc[acc_rows(core, rel, part), :] + precv[rel, part].astype(F32)
        ).astype(BF16)
        xc[rel, part] = send(
            remote(
                xsend.at[rel, part], xrecv.at[1 - rel, part], x_send.at[rel, part], x_recv.at[1 - rel, part], peers[1]
            )
        )

    def arrived(rel, part):
        remote(
            xsend.at[rel, part], xrecv.at[rel, part], x_send.at[rel, part], x_recv.at[rel, part], peers[1]
        ).wait_recv()

    w_relay(0, (1, 2, 3))
    w_ready(0, (0,))
    for c in bc:
        c.wait_recv()

    ones = jnp.ones((NBLK * BLK, cols), BF16)
    lane = lax.broadcasted_iota(jnp.int32, (BLK, cols), 1) // HEAD_DIM
    block_count = local_blocks * n_dom

    def kv_index(b, t):
        away = nbr[b, t] - (dom * local_blocks - HB)
        away = jnp.where(away < 0, away + block_count, away)
        away = jnp.where(away >= block_count, away - block_count, away)
        away = jnp.minimum(away, local_blocks + 2 * HB - 1)
        o = away % n_mp
        role = ((o // 2 + side) % 2) * 2 + (o % 2 + core) % 2
        return role * span + away // n_mp

    cc, hc, rc, nc = {}, {}, {}, {}

    def spread(l, q, part):
        cc[q, part] = send(
            remote(
                nown.at[l, q, part], nown.at[l, q + 1, part], c_send.at[l, q // 2, part], c_recv.at[l, q // 2, part], peers[0]
            )
        )
        if part == 0:
            for s in range(2):
                hc[s, q] = send(
                    remote(
                        nown.at[l, q, 0, pl.ds(s * edge * BLK, edge * BLK)],
                        nhalo.at[l, 1 - s, q],
                        h_send.at[l, s, q // 2],
                        h_recv.at[l, 1 - s, q // 2],
                        beside[s],
                    )
                )

    def halo_arrived(l, s, q):
        remote(
            nhalo.at[l, s, q], nhalo.at[l, s, q], h_send.at[l, s, q // 2], h_recv.at[l, s, q // 2], beside[0]
        ).wait_recv()

    def relay_halo(l, s, q):
        rc[s, q] = send(
            remote(
                nhalo.at[l, s, q], nhalo.at[l, s, q + 1], r_send.at[l, s, q // 2], r_recv.at[l, s, q // 2], peers[0]
            )
        )

    def joined(l, c):
        return jnp.concatenate([gq[l, r, c] for r in range(n_mp)], axis=1)

    def project(l, found):
        x = jnp.concatenate([f[0] for f in found], axis=0)
        k = mm(x, joined(l, 1)).astype(BF16)
        v = mm(x, joined(l, 2)).astype(BF16)
        spots = [role * span + w for f in found for role, w in [(f[1], w) for w in f[2]]]
        for j, w in enumerate(spots):
            kbuf[w] = k[j * BLK : (j + 1) * BLK]
            vbuf[w] = v[j * BLK : (j + 1) * BLK]

    def own_part(l, role, part):
        n = per // 2
        return (nown[l, role, part], role, [edge + i for i in order_of[part * n : (part + 1) * n]])

    def halo_part(l, s, role):
        return (nhalo[l, s, role], role, [s * (span - edge) + i for i in range(edge)])

    def attend(l):
        for r, i in enumerate(order_of):
            b = i * n_mp + m
            index = [kv_index(b, t) for t in range(NBLK)]
            for p in range(n_mp):
                at = slice(p * cols, (p + 1) * cols)
                q = qs[r * BLK : (r + 1) * BLK, at]
                qbd = jnp.concatenate(
                    [jnp.where(lane == h, q.astype(F32), 0.0) for h in range(heads)], axis=0
                ).astype(BF16)
                keys = jnp.concatenate([kbuf[j, :, at] for j in index], axis=0)
                values = jnp.concatenate(
                    [jnp.concatenate([vbuf[j, :, at] for j in index], axis=0), ones], axis=1
                )
                lean = bias[m, r] if p == 0 else brecv[p - 1, r]
                s = dot_nt(keys, qbd).reshape(NBLK, BLK, heads * BLK) + lean[:, None, :]
                s = s.reshape(NBLK * BLK, heads * BLK)
                e = jnp.exp2(s - jnp.max(s, axis=0, keepdims=True)).astype(BF16)
                o = dot_tn(e, values)
                o = o[:, 0:cols] / o[:, cols : 2 * cols]
                merged = o[0:BLK]
                for h in range(1, heads):
                    merged = jnp.where(lane == h, o[h * BLK : (h + 1) * BLK], merged)
                att[r * BLK : (r + 1) * BLK, at] = merged.astype(BF16)

    for l in range(layers):
        gain = ln_gain[l, 0:1, :]
        if l == 0:
            def settle(rel, part):
                arrived(rel, part)
                x = (xsend[rel, part].astype(F32) + xrecv[rel, part].astype(F32)).astype(BF16)
                if rel == 0:
                    xown[part * prow : (part + 1) * prow] = x
                nown[0, 2 * rel, part] = normalize(x.astype(F32), gain).astype(BF16)
                spread(0, 2 * rel, part)

            settle(1, 0)
            settle(0, 0)
            project(l, [own_part(l, 0, 0), own_part(l, 2, 0)])
            settle(1, 1)
        else:
            for part in range(2):
                x = xown[part * prow : (part + 1) * prow].astype(F32)
                nown[l, 0, part] = normalize(x, gain).astype(BF16)
                nc[part] = send(
                    remote(
                        nown.at[l, 0, part], nown.at[l, 2, part], n_send.at[l, part], n_recv.at[l, part], peers[1]
                    )
                )
                spread(l, 0, part)
            w_ready(l, (0,))
            project(l, [own_part(l, 0, 0), own_part(l, 0, 1)])
            nc[0].wait_recv()
            spread(l, 2, 0)
        for q in (2, 0):
            cc[q, 0].wait_recv()
        if l == 0:
            project(l, [own_part(l, 1, 0), own_part(l, 3, 0)])
            settle(0, 1)
            project(l, [own_part(l, 0, 1), own_part(l, 2, 1)])
        else:
            project(l, [own_part(l, 2, 0), own_part(l, 1, 0), own_part(l, 3, 0)])
            nc[1].wait_recv()
            spread(l, 2, 1)
        x = jnp.concatenate([nown[l, 0, 0], nown[l, 0, 1]], axis=0)
        qs[...] = (mm(x, joined(l, 0)) * (HEAD_DIM ** (-0.5) * LOG2E)).astype(BF16)
        if l == 0:
            w_relay(1, (0,))
        for q in (0, 2):
            for s in range(2):
                halo_arrived(l, s, q)
                relay_halo(l, s, q)
        for q in (0, 2):
            cc[q, 1].wait_recv()
        if l == 0:
            rest = [own_part(l, 1, 1), own_part(l, 3, 1)]
        else:
            rest = [own_part(l, 2, 1), own_part(l, 1, 1), own_part(l, 3, 1)]
        project(l, rest + [halo_part(l, s, q) for q in (0, 2) for s in range(2)])
        for key in rc:
            rc[key].wait_recv()
        project(l, [halo_part(l, s, q + 1) for q in (0, 2) for s in range(2)])
        if l == 0:
            w_forward(1, (1, 2))
            w_start(0, 1, (3,))
        else:
            w_forward(l, (3,))
            w_relay(l, (1, 2))
        attend(l)
        if l > 0:
            w_relay(l, (3,))
        w_ready(l, (1, 2, 3))
        mixed = jnp.concatenate([gout[l, r] for r in range(n_mp)], axis=0)
        x1 = (xown[...].astype(F32) + mm(att[...], mixed)).astype(BF16).astype(F32)
        n2 = normalize(x1, ln_gain[l, 1:2, :]).astype(BF16)
        total = x1
        for r in range(n_mp):
            total = total + mm(silu(mm(n2, gup[l, r])).astype(BF16), gdown[l, r])
        if l + 1 < layers:
            xown[...] = total.astype(BF16)
        else:
            for r, i in enumerate(order_of):
                fin[i] = total[r * BLK : (r + 1) * BLK].astype(BF16)

    fc = []
    for k in (1, 2, 0):
        there = peers[k][1]
        fc.append(
            send(
                remote(
                    fin.at[:, :, pl.ds(pl.multiple_of(there * cols, cols), cols)],
                    result.at[:, m],
                    f_send.at[k],
                    f_recv.at[k],
                    peers[k],
                )
            )
        )
    result[:, m] = fin[:, :, my_cols]
    for n in far:
        for c in moving[n]:
            c.wait_send()
    for c in sent:
        c.wait_send()
    for c in fc:
        c.wait_recv()


def shards(
    grid_feat,
    grid_target,
    enc_w1,
    enc_b1,
    enc_w2,
    enc_gain,
    mesh_embed,
    nbr_blocks,
    attn_bias,
    ln_gain,
    qkv_w,
    out_w,
    up_w,
    down_w,
):
    n_dom = lax.axis_size("dom")
    n_mp = lax.axis_size("mp")
    rows, f_in = grid_feat.shape
    width = enc_w2.shape[1]
    cols = width // n_mp
    nodes = mesh_embed.shape[0]
    heads = cols // HEAD_DIM
    layers = ln_gain.shape[0]
    cap = 2 * rows // n_dom
    per = nodes // BLK // n_mp
    edge = HB // n_mp
    prow = per // 2 * BLK
    ff = up_w.shape[2]
    vmem = pl.BlockSpec(memory_space=pltpu.VMEM)
    dma = pltpu.SemaphoreType.DMA
    out = pl.pallas_call(
        functools.partial(mega, n_dom, n_mp, layers),
        out_shape=jax.ShapeDtypeStruct((per, n_mp, BLK, cols), BF16),
        in_specs=[pl.BlockSpec(memory_space=pltpu.SMEM)] + [vmem] * 9 + [pl.BlockSpec(memory_space=pl.ANY)] * 4,
        out_specs=vmem,
        scratch_shapes=[
            pltpu.VMEM((n_mp, per, NBLK, heads * BLK), F32),
            pltpu.VMEM((3, per, NBLK, heads * BLK), F32),
            pltpu.VMEM((n_dom, cap, f_in), BF16),
            pltpu.VMEM((n_dom, 1, cap), jnp.int32),
            pltpu.VMEM((n_dom, cap, f_in), BF16),
            pltpu.VMEM((n_dom, 1, cap), jnp.int32),
            pltpu.VMEM((nodes, width), F32),
            pltpu.VMEM((2, 2, prow, width), BF16),
            pltpu.VMEM((2, 2, prow, width), BF16),
            pltpu.VMEM((2, 2, prow, width), BF16),
            pltpu.VMEM((2, 2, prow, width), BF16),
            pltpu.VMEM((per * BLK, width), BF16),
            pltpu.VMEM((layers, n_mp, 2, prow, width), BF16),
            pltpu.VMEM((layers, 2, n_mp, edge * BLK, width), BF16),
            pltpu.VMEM((n_mp * (per + 2 * edge), BLK, width), BF16),
            pltpu.VMEM((n_mp * (per + 2 * edge), BLK, width), BF16),
            pltpu.VMEM((per * BLK, width), BF16),
            pltpu.VMEM((per * BLK, width), BF16),
            pltpu.VMEM((layers, n_mp) + qkv_w.shape[1:], BF16),
            pltpu.VMEM((layers, n_mp) + out_w.shape[1:], BF16),
            pltpu.VMEM((layers, n_mp, width, ff), BF16),
            pltpu.VMEM((layers, n_mp, ff, width), BF16),
            pltpu.VMEM((per, BLK, width), BF16),
            dma((2, n_dom)),
            dma((2, n_dom)),
            dma((3,)),
            dma((3,)),
            dma((2, 2)),
            dma((2, 2)),
            dma((2, 2)),
            dma((2, 2)),
            dma((layers, 2)),
            dma((layers, 2)),
            dma((layers, 2, 2)),
            dma((layers, 2, 2)),
            dma((layers, 2, 2)),
            dma((layers, 2, 2)),
            dma((layers, 2, 2)),
            dma((layers, 2, 2)),
            dma((5, layers, 4)),
            dma((5, layers, 4)),
            dma((3,)),
            dma((3,)),
            dma((layers, 4)),
        ],
        compiler_params=pltpu.CompilerParams(
            collective_id=0, has_side_effects=True, vmem_limit_bytes=60 * 1024 * 1024
        ),
    )(
        nbr_blocks,
        grid_feat,
        grid_target.reshape(1, rows),
        enc_w1,
        enc_b1.reshape(1, width),
        enc_w2,
        enc_gain.reshape(1, width),
        mesh_embed,
        attn_bias,
        ln_gain,
        qkv_w,
        out_w,
        up_w,
        down_w,
    )
    return out.reshape(nodes, cols)


def solution(mesh):
    placed = (
        P(("dom", "mp"), None),
        P(("dom", "mp")),
        P(),
        P(),
        P(),
        P(),
        P("dom", "mp"),
        P("dom", None),
        P("mp", None, "dom"),
        P(),
        P(None, None, None, "mp"),
        P(None, "mp", None),
        P(None, None, "mp"),
        P(None, "mp", None),
    )
    return jax.shard_map(
        shards, mesh=mesh, in_specs=placed, out_specs=P("dom", "mp"), check_vma=False
    )
```

```python
import functools

import jax
import jax.numpy as jnp
from jax import lax
from jax.experimental import pallas as pl
from jax.experimental.pallas import tpu as pltpu
from jax.sharding import PartitionSpec as P

HEAD_DIM = 64
BLK = 64
NBLK = 16
HB = 4
EPS = 1e-05
LOG2E = 1.4426950408889634
LEADS = (0, 1, 0, 1)
CUTS = ((1, 2, 2, 4), (4, 4, 4, 4))
F32 = jnp.float32
BF16 = jnp.bfloat16
MESH = pl.DeviceIdType.MESH


def normalize(values, gain_row):
    row_mean = jnp.mean(values, axis=-1, keepdims=True)
    centered = values - row_mean
    variance = jnp.mean(centered * centered, axis=-1, keepdims=True)
    return centered * lax.rsqrt(variance + EPS) * gain_row


def silu(v):
    return v / (1.0 + jnp.exp(-v))


def mm(a, b):
    return jnp.dot(a, b, preferred_element_type=F32)


def dot_nt(a, b):
    return lax.dot_general(a, b, (((1,), (1,)), ((), ())), preferred_element_type=F32)


def dot_tn(a, b):
    return lax.dot_general(a, b, (((0,), (0,)), ((), ())), preferred_element_type=F32)


def remote(src, dst, send, recv, where):
    return pltpu.make_async_remote_copy(
        src, dst, send, recv, device_id=where, device_id_type=MESH
    )


def mega(
    n_dom,
    n_mp,
    layers,
    nbr,
    feat_hbm,
    target_hbm,
    w1_hbm,
    b1_hbm,
    w2_hbm,
    egain_hbm,
    embed_hbm,
    bias_hbm,
    ln_hbm,
    qkv_hbm,
    out_hbm,
    up_hbm,
    down_hbm,
    result,
    feat,
    target,
    w1,
    b1,
    w2,
    egain,
    embed,
    bias_in,
    ln_gain,
    i_sem,
    bias,
    brecv,
    sbuf,
    sland,
    rbuf,
    rland,
    acc,
    psend,
    precv,
    xsend,
    xrecv,
    xown,
    nown,
    nhalo,
    kbuf,
    vbuf,
    qs,
    att,
    gq,
    gout,
    gup,
    gdown,
    fin,
    d_send,
    d_recv,
    b_send,
    b_recv,
    p_send,
    p_recv,
    x_send,
    x_recv,
    n_send,
    n_recv,
    c_send,
    c_recv,
    h_send,
    h_recv,
    r_send,
    r_recv,
    w_send,
    w_recv,
    f_send,
    f_recv,
    l_sem,
):
    dom = lax.axis_index("dom")
    m = lax.axis_index("mp")
    rows = feat.shape[0]
    cap = sbuf.shape[1]
    nodes, width = acc.shape
    cols = embed.shape[1]
    heads = cols // HEAD_DIM
    local_blocks = nodes // BLK
    per = local_blocks // n_mp
    edge = HB // n_mp
    span = per + 2 * edge
    prow = per // 2 * BLK
    core, side = m % 2, m // 2
    order_of = list(range(edge)) + list(range(per - edge, per)) + list(range(edge, per - edge))
    mine = (dom, m)
    peers = [(dom, m + 1 - 2 * (m % 2)), (dom, (m + 2) % 4), (dom, 3 - m)]
    beside = [((dom + n_dom - 1) % n_dom, m), ((dom + 1) % n_dom, m)]

    def across(n):
        e = 0
        bit = 1
        while bit < n_dom:
            own = (dom // bit) % 2
            e = e + ((1 - own) if n & bit else own) * bit
            bit *= 2
        return e

    barrier = pltpu.get_barrier_semaphore()
    for n in range(1, n_dom):
        pl.semaphore_signal(barrier, inc=1, device_id=(across(n), m), device_id_type=MESH)
    for p in peers:
        pl.semaphore_signal(barrier, inc=1, device_id=p, device_id_type=MESH)

    inputs = [
        pltpu.make_async_copy(src, dst, i_sem.at[j])
        for j, (src, dst) in enumerate(
            (
                (target_hbm, target),
                (feat_hbm, feat),
                (w1_hbm, w1),
                (b1_hbm, b1),
                (w2_hbm, w2),
                (egain_hbm, egain),
                (bias_hbm, bias_in),
                (embed_hbm, embed),
                (ln_hbm, ln_gain),
            )
        )
    ]
    for c in inputs:
        c.start()
    inputs[0].wait()

    owner = target[...] // nodes
    node = target[...] % nodes
    block = node // BLK
    held_by = block % n_mp
    nth = block // n_mp
    nth = jnp.where(
        nth < edge, nth, jnp.where(nth >= per - edge, nth - (per - 2 * edge), nth + edge)
    )
    place = (((held_by % 2) * 2 + held_by // 2) * per + nth) * BLK + node % BLK
    member = (lax.broadcasted_iota(jnp.int32, (n_dom, rows), 0) == owner).astype(F32)
    lanes = 128
    chunks = rows // lanes
    stacked = jnp.concatenate(
        [member[:, j * lanes : (j + 1) * lanes] for j in range(chunks)], axis=0
    ).astype(BF16)
    row_i = lax.broadcasted_iota(jnp.int32, (lanes, 2 * lanes), 0)
    col_i = lax.broadcasted_iota(jnp.int32, (lanes, 2 * lanes), 1)
    before = ((row_i < col_i) | (col_i >= lanes)).astype(F32).astype(BF16)
    counts = mm(stacked, before)
    running = jnp.zeros((n_dom, lanes), F32)
    ranks = []
    for j in range(chunks):
        part = counts[j * n_dom : (j + 1) * n_dom]
        here = (part[:, 0:lanes] + running) * member[:, j * lanes : (j + 1) * lanes]
        ranks.append(jnp.sum(here, axis=0, keepdims=True))
        running = running + part[:, lanes:]
    rank = jnp.concatenate(ranks, axis=1)
    hi = (place // 32).astype(F32)
    lo = (place % 32).astype(F32)
    pick = lax.broadcasted_iota(jnp.int32, (16, rows), 0)
    parts = jnp.where(
        pick == 0, hi, jnp.where(pick == 1, lo, jnp.where(pick == 2, 1.0, 0.0))
    ).astype(BF16)
    inputs[1].wait()
    features = feat[...]
    seat = lax.broadcasted_iota(jnp.int32, (cap, rows), 0).astype(F32).astype(BF16)

    def outgoing(n):
        wanted = jnp.where(owner == across(n), rank, -1.0).astype(BF16)
        here = jnp.where(seat == wanted, jnp.ones((), BF16), jnp.zeros((), BF16))
        sbuf[n] = mm(here, features).astype(BF16)
        where_to = dot_nt(parts, here)
        landed = where_to[0:1] * 32.0 + where_to[1:2]
        sland[n] = jnp.where(where_to[2:3] > 0.5, landed, -1.0).astype(jnp.int32)

    def d_copies(n):
        there = (across(n), m)
        return [
            remote(sbuf.at[n], rbuf.at[n], d_send.at[0, n], d_recv.at[0, n], there),
            remote(sland.at[n], rland.at[n], d_send.at[1, n], d_recv.at[1, n], there),
        ]

    def start_all(copies):
        for c in copies:
            c.start()

    sent = []

    def send(c):
        c.start()
        sent.append(c)
        return c

    arrays = ((qkv_hbm, gq), (out_hbm, gout), (up_hbm, gup), (down_hbm, gdown))
    bits = (dom % 2, (dom // 2) % 2)
    twins = ((dom + 1 - 2 * bits[0], m), (dom + 2 - 4 * bits[1], m))

    def part_of(ref, lead, i, h, cuts):
        size = ref.shape[-2] // cuts
        at = pl.ds(pl.multiple_of(h * size, size), size)
        return ref.at[lead + ((slice(None), at) if i == 0 else (at,))]

    def w_copy(k, l, i):
        own, got = arrays[i]
        first = LEADS[i]
        half = bits[1 - first]
        quarter = bits[first] + 2 * half
        cuts = CUTS[min(l, 1)][i]
        sems = (w_send.at[k, l, i], w_recv.at[k, l, i])
        if k == 0:
            h = (0, half, quarter)[cuts // 2]
            return remote(
                part_of(own, (l,), i, h, cuts), part_of(got, (l, 2), i, h, cuts), *sems, peers[1]
            )
        if k == 1:
            piece = part_of(got, (l, 2), i, quarter, 4)
            return remote(piece, piece, *sems, twins[first])
        if k == 2:
            return remote(own.at[l], got.at[l, 1], *sems, peers[0])
        if k == 5:
            piece = part_of(got, (l, 2), i, half, 2)
            return remote(piece, piece, *sems, twins[1 - first])
        if cuts == 1:
            return remote(got.at[l, 2], got.at[l, 3], *sems, peers[0])
        h = half if k == 3 else 1 - half
        return remote(part_of(got, (l, 2), i, h, 2), part_of(got, (l, 3), i, h, 2), *sems, peers[0])

    wc = {}

    def w_start(k, l, ids):
        if l < layers:
            for i in ids:
                wc[k, l, i] = send(w_copy(k, l, i))

    def w_next(k, l, ids):
        if l < layers:
            for i in ids:
                if (k, l, i) not in wc:
                    continue
                wc[k, l, i].wait_recv()
                after = {1: (5, 3), 5: (4,)}
                after[0] = {1: (3,), 2: (5, 3), 4: (1,)}[CUTS[min(l, 1)][i]]
                for j in after[k]:
                    w_start(j, l, (i,))

    def w_ready(l, ids):
        for i in ids:
            local[l, i].wait()
            for k in (2, 3, 4):
                if (k, l, i) in wc:
                    wc[k, l, i].wait_recv()

    local = {
        (l, i): pltpu.make_async_copy(own.at[l], got.at[l, 0], l_sem.at[l, i])
        for l in range(layers)
        for i, (own, got) in enumerate(arrays)
    }

    far = list(range(n_dom - 1, 0, -1))
    outgoing(far[0])
    pl.semaphore_wait(barrier, n_dom - 1 + len(peers))
    w_start(0, 0, (0,))
    moving = {}
    for j, n in enumerate(far):
        if j:
            outgoing(n)
        moving[n] = d_copies(n)
        start_all(moving[n])
    w_start(0, 0, (1, 2, 3))
    for c in inputs[2:]:
        c.wait()
    for l in range(layers):
        w_start(2, l, (0, 1, 2, 3))
    for key in local:
        local[key].start()
    for o in range(n_mp):
        for r, i in enumerate(order_of):
            b = i * n_mp + o
            bias[o, r] = LOG2E * jnp.concatenate(
                [bias_in[h, :, b * BLK : (b + 1) * BLK] for h in range(heads)], axis=1
            )
    bc = [
        send(remote(bias.at[peers[k][1]], brecv.at[k], b_send.at[k], b_recv.at[k], peers[k]))
        for k in range(3)
    ]
    outgoing(0)

    def consume(buf, land, first):
        v = mm(buf, w1[...]) + b1[...]
        message = normalize(mm(silu(v).astype(BF16), w2[...]), egain[...]).astype(BF16)
        step = cap
        spot = lax.broadcasted_iota(jnp.int32, (step, cap), 0).astype(F32).astype(BF16)
        for c in range(nodes // step):
            goal = (land - c * step).astype(F32).astype(BF16)
            scatter = jnp.where(spot == goal, jnp.ones((), BF16), jnp.zeros((), BF16))
            at = slice(c * step, (c + 1) * step)
            if first:
                acc[at] = mm(scatter, message)
            else:
                acc[at] += mm(scatter, message)

    consume(sbuf[0], sland[0], True)
    my_cols = pl.ds(pl.multiple_of(m * cols, cols), cols)
    for o in range(n_mp):
        for r, i in enumerate(order_of):
            b = i * n_mp + o
            at = (((o % 2) * 2 + o // 2) * per + r) * BLK
            acc[at : at + BLK, my_cols] += embed[b * BLK : (b + 1) * BLK].astype(F32)
    w_start(0, 1, (0, 1, 2, 3))
    near = list(range(1, n_dom // 2))
    late = list(range(n_dom - 1, n_dom // 2 - 1, -1))
    for j, n in enumerate(near + late):
        for c in moving[n]:
            c.wait_recv()
        consume(rbuf[n], rland[n], False)
        if j == len(near) + len(late) // 2 - 1:
            w_next(0, 0, (0,))

    def acc_rows(c, rel, part):
        at = (c * 2 + (side + rel) % 2) * per * BLK + part * prow
        return pl.ds(pl.multiple_of(at, BLK), prow)

    pieces = [(0, 0), (1, 0), (0, 1), (1, 1)]
    pc = {}
    for rel, part in pieces:
        psend[rel, part] = acc[acc_rows(1 - core, rel, part), :].astype(BF16)
        pc[rel, part] = send(
            remote(psend.at[rel, part], precv.at[rel, part], p_send.at[rel, part], p_recv.at[rel, part], peers[0])
        )
    w_next(0, 0, (1, 2, 3))
    xc = {}
    for rel, part in pieces:
        pc[rel, part].wait_recv()
        xsend[rel, part] = (
            acc[acc_rows(core, rel, part), :] + precv[rel, part].astype(F32)
        ).astype(BF16)
        xc[rel, part] = send(
            remote(
                xsend.at[rel, part], xrecv.at[1 - rel, part], x_send.at[rel, part], x_recv.at[1 - rel, part], peers[1]
            )
        )

    def arrived(rel, part):
        remote(
            xsend.at[rel, part], xrecv.at[rel, part], x_send.at[rel, part], x_recv.at[rel, part], peers[1]
        ).wait_recv()

    w_next(0, 1, (0, 1, 2, 3))
    w_ready(0, (0,))
    for c in bc:
        c.wait_recv()

    ones = jnp.ones((NBLK * BLK, cols), BF16)
    lane = lax.broadcasted_iota(jnp.int32, (BLK, cols), 1) // HEAD_DIM
    block_count = local_blocks * n_dom

    def kv_index(b, t):
        away = nbr[b, t] - (dom * local_blocks - HB)
        away = jnp.where(away < 0, away + block_count, away)
        away = jnp.where(away >= block_count, away - block_count, away)
        away = jnp.minimum(away, local_blocks + 2 * HB - 1)
        o = away % n_mp
        role = ((o // 2 + side) % 2) * 2 + (o % 2 + core) % 2
        return role * span + away // n_mp

    cc, hc, rc, nc = {}, {}, {}, {}

    def spread(l, q, part):
        cc[q, part] = send(
            remote(
                nown.at[l, q, part], nown.at[l, q + 1, part], c_send.at[l, q // 2, part], c_recv.at[l, q // 2, part], peers[0]
            )
        )
        if part == 0:
            for s in range(2):
                hc[s, q] = send(
                    remote(
                        nown.at[l, q, 0, pl.ds(s * edge * BLK, edge * BLK)],
                        nhalo.at[l, 1 - s, q],
                        h_send.at[l, s, q // 2],
                        h_recv.at[l, 1 - s, q // 2],
                        beside[s],
                    )
                )

    def halo_arrived(l, s, q):
        remote(
            nhalo.at[l, s, q], nhalo.at[l, s, q], h_send.at[l, s, q // 2], h_recv.at[l, s, q // 2], beside[0]
        ).wait_recv()

    def relay_halo(l, s, q):
        rc[s, q] = send(
            remote(
                nhalo.at[l, s, q], nhalo.at[l, s, q + 1], r_send.at[l, s, q // 2], r_recv.at[l, s, q // 2], peers[0]
            )
        )

    def joined(l, c):
        return jnp.concatenate([gq[l, r, c] for r in range(n_mp)], axis=1)

    def project(l, found):
        x = jnp.concatenate([f[0] for f in found], axis=0)
        k = mm(x, joined(l, 1)).astype(BF16)
        v = mm(x, joined(l, 2)).astype(BF16)
        spots = [role * span + w for f in found for role, w in [(f[1], w) for w in f[2]]]
        for j, w in enumerate(spots):
            kbuf[w] = k[j * BLK : (j + 1) * BLK]
            vbuf[w] = v[j * BLK : (j + 1) * BLK]

    def own_part(l, role, part):
        n = per // 2
        return (nown[l, role, part], role, [edge + i for i in order_of[part * n : (part + 1) * n]])

    def halo_part(l, s, role):
        return (nhalo[l, s, role], role, [s * (span - edge) + i for i in range(edge)])

    def attend(l):
        for r, i in enumerate(order_of):
            b = i * n_mp + m
            index = [kv_index(b, t) for t in range(NBLK)]
            for p in range(n_mp):
                at = slice(p * cols, (p + 1) * cols)
                q = qs[r * BLK : (r + 1) * BLK, at]
                qbd = jnp.concatenate(
                    [jnp.where(lane == h, q.astype(F32), 0.0) for h in range(heads)], axis=0
                ).astype(BF16)
                keys = jnp.concatenate([kbuf[j, :, at] for j in index], axis=0)
                values = jnp.concatenate(
                    [jnp.concatenate([vbuf[j, :, at] for j in index], axis=0), ones], axis=1
                )
                lean = bias[m, r] if p == 0 else brecv[p - 1, r]
                s = dot_nt(keys, qbd).reshape(NBLK, BLK, heads * BLK) + lean[:, None, :]
                s = s.reshape(NBLK * BLK, heads * BLK)
                e = jnp.exp2(s - jnp.max(s, axis=0, keepdims=True)).astype(BF16)
                o = dot_tn(e, values)
                o = o[:, 0:cols] / o[:, cols : 2 * cols]
                merged = o[0:BLK]
                for h in range(1, heads):
                    merged = jnp.where(lane == h, o[h * BLK : (h + 1) * BLK], merged)
                att[r * BLK : (r + 1) * BLK, at] = merged.astype(BF16)

    for l in range(layers):
        gain = ln_gain[l, 0:1, :]
        if l == 0:
            def settle(rel, part):
                arrived(rel, part)
                x = (xsend[rel, part].astype(F32) + xrecv[rel, part].astype(F32)).astype(BF16)
                if rel == 0:
                    xown[part * prow : (part + 1) * prow] = x
                nown[0, 2 * rel, part] = normalize(x.astype(F32), gain).astype(BF16)
                spread(0, 2 * rel, part)

            settle(1, 0)
            w_next(1, 0, (1, 2, 3))
            settle(0, 0)
            project(l, [own_part(l, 0, 0), own_part(l, 2, 0)])
            settle(1, 1)
        else:
            for part in range(2):
                x = xown[part * prow : (part + 1) * prow].astype(F32)
                nown[l, 0, part] = normalize(x, gain).astype(BF16)
                nc[part] = send(
                    remote(
                        nown.at[l, 0, part], nown.at[l, 2, part], n_send.at[l, part], n_recv.at[l, part], peers[1]
                    )
                )
                spread(l, 0, part)
            w_next(5, l, (0,))
            w_ready(l, (0,))
            project(l, [own_part(l, 0, 0), own_part(l, 0, 1)])
            nc[0].wait_recv()
            spread(l, 2, 0)
        for q in (2, 0):
            cc[q, 0].wait_recv()
        if l == 0:
            project(l, [own_part(l, 1, 0), own_part(l, 3, 0)])
            settle(0, 1)
            project(l, [own_part(l, 0, 1), own_part(l, 2, 1)])
        else:
            project(l, [own_part(l, 2, 0), own_part(l, 1, 0), own_part(l, 3, 0)])
            nc[1].wait_recv()
            spread(l, 2, 1)
        x = jnp.concatenate([nown[l, 0, 0], nown[l, 0, 1]], axis=0)
        qs[...] = (mm(x, joined(l, 0)) * (HEAD_DIM ** (-0.5) * LOG2E)).astype(BF16)
        for q in (0, 2):
            for s in range(2):
                halo_arrived(l, s, q)
                relay_halo(l, s, q)
        w_next(5, l, (1, 2, 3))
        for q in (0, 2):
            cc[q, 1].wait_recv()
        if l == 0:
            rest = [own_part(l, 1, 1), own_part(l, 3, 1)]
        else:
            rest = [own_part(l, 2, 1), own_part(l, 1, 1), own_part(l, 3, 1)]
        project(l, rest + [halo_part(l, s, q) for q in (0, 2) for s in range(2)])
        for key in rc:
            rc[key].wait_recv()
        project(l, [halo_part(l, s, q + 1) for q in (0, 2) for s in range(2)])
        if l == 0:
            w_next(1, 1, (0, 1, 2, 3))
        attend(l)
        w_ready(l, (1, 2, 3))
        mixed = jnp.concatenate([gout[l, r] for r in range(n_mp)], axis=0)
        x1 = (xown[...].astype(F32) + mm(att[...], mixed)).astype(BF16).astype(F32)
        n2 = normalize(x1, ln_gain[l, 1:2, :]).astype(BF16)
        total = x1
        for r in range(n_mp):
            total = total + mm(silu(mm(n2, gup[l, r])).astype(BF16), gdown[l, r])
        if l + 1 < layers:
            xown[...] = total.astype(BF16)
        else:
            for r, i in enumerate(order_of):
                fin[i] = total[r * BLK : (r + 1) * BLK].astype(BF16)

    fc = []
    for k in (1, 2, 0):
        there = peers[k][1]
        fc.append(
            send(
                remote(
                    fin.at[:, :, pl.ds(pl.multiple_of(there * cols, cols), cols)],
                    result.at[:, m],
                    f_send.at[k],
                    f_recv.at[k],
                    peers[k],
                )
            )
        )
    result[:, m] = fin[:, :, my_cols]
    for n in far:
        for c in moving[n]:
            c.wait_send()
    for c in sent:
        c.wait_send()
    for c in fc:
        c.wait_recv()


def shards(
    grid_feat,
    grid_target,
    enc_w1,
    enc_b1,
    enc_w2,
    enc_gain,
    mesh_embed,
    nbr_blocks,
    attn_bias,
    ln_gain,
    qkv_w,
    out_w,
    up_w,
    down_w,
):
    n_dom = lax.axis_size("dom")
    n_mp = lax.axis_size("mp")
    rows, f_in = grid_feat.shape
    width = enc_w2.shape[1]
    cols = width // n_mp
    nodes = mesh_embed.shape[0]
    heads = cols // HEAD_DIM
    layers = ln_gain.shape[0]
    cap = 2 * rows // n_dom
    per = nodes // BLK // n_mp
    edge = HB // n_mp
    prow = per // 2 * BLK
    ff = up_w.shape[2]
    vmem = pl.BlockSpec(memory_space=pltpu.VMEM)
    dma = pltpu.SemaphoreType.DMA
    out = pl.pallas_call(
        functools.partial(mega, n_dom, n_mp, layers),
        out_shape=jax.ShapeDtypeStruct((per, n_mp, BLK, cols), BF16),
        in_specs=[pl.BlockSpec(memory_space=pltpu.SMEM)] + [pl.BlockSpec(memory_space=pl.ANY)] * 13,
        out_specs=vmem,
        scratch_shapes=[
            pltpu.VMEM(grid_feat.shape, BF16),
            pltpu.VMEM((1, rows), jnp.int32),
            pltpu.VMEM(enc_w1.shape, BF16),
            pltpu.VMEM((1, width), F32),
            pltpu.VMEM(enc_w2.shape, BF16),
            pltpu.VMEM((1, width), F32),
            pltpu.VMEM(mesh_embed.shape, BF16),
            pltpu.VMEM(attn_bias.shape, F32),
            pltpu.VMEM(ln_gain.shape, F32),
            dma((9,)),
            pltpu.VMEM((n_mp, per, NBLK, heads * BLK), F32),
            pltpu.VMEM((3, per, NBLK, heads * BLK), F32),
            pltpu.VMEM((n_dom, cap, f_in), BF16),
            pltpu.VMEM((n_dom, 1, cap), jnp.int32),
            pltpu.VMEM((n_dom, cap, f_in), BF16),
            pltpu.VMEM((n_dom, 1, cap), jnp.int32),
            pltpu.VMEM((nodes, width), F32),
            pltpu.VMEM((2, 2, prow, width), BF16),
            pltpu.VMEM((2, 2, prow, width), BF16),
            pltpu.VMEM((2, 2, prow, width), BF16),
            pltpu.VMEM((2, 2, prow, width), BF16),
            pltpu.VMEM((per * BLK, width), BF16),
            pltpu.VMEM((layers, n_mp, 2, prow, width), BF16),
            pltpu.VMEM((layers, 2, n_mp, edge * BLK, width), BF16),
            pltpu.VMEM((n_mp * (per + 2 * edge), BLK, width), BF16),
            pltpu.VMEM((n_mp * (per + 2 * edge), BLK, width), BF16),
            pltpu.VMEM((per * BLK, width), BF16),
            pltpu.VMEM((per * BLK, width), BF16),
            pltpu.VMEM((layers, n_mp) + qkv_w.shape[1:], BF16),
            pltpu.VMEM((layers, n_mp) + out_w.shape[1:], BF16),
            pltpu.VMEM((layers, n_mp, width, ff), BF16),
            pltpu.VMEM((layers, n_mp, ff, width), BF16),
            pltpu.VMEM((per, BLK, width), BF16),
            dma((2, n_dom)),
            dma((2, n_dom)),
            dma((3,)),
            dma((3,)),
            dma((2, 2)),
            dma((2, 2)),
            dma((2, 2)),
            dma((2, 2)),
            dma((layers, 2)),
            dma((layers, 2)),
            dma((layers, 2, 2)),
            dma((layers, 2, 2)),
            dma((layers, 2, 2)),
            dma((layers, 2, 2)),
            dma((layers, 2, 2)),
            dma((layers, 2, 2)),
            dma((6, layers, 4)),
            dma((6, layers, 4)),
            dma((3,)),
            dma((3,)),
            dma((layers, 4)),
        ],
        compiler_params=pltpu.CompilerParams(
            collective_id=0, has_side_effects=True, vmem_limit_bytes=60 * 1024 * 1024
        ),
    )(
        nbr_blocks,
        grid_feat,
        grid_target.reshape(1, rows),
        enc_w1,
        enc_b1.reshape(1, width),
        enc_w2,
        enc_gain.reshape(1, width),
        mesh_embed,
        attn_bias,
        ln_gain,
        qkv_w,
        out_w,
        up_w,
        down_w,
    )
    return out.reshape(nodes, cols)


def solution(mesh):
    placed = (
        P(("dom", "mp"), None),
        P(("dom", "mp")),
        P(),
        P(),
        P(),
        P(),
        P("dom", "mp"),
        P("dom", None),
        P("mp", None, "dom"),
        P(),
        P(None, None, None, "mp"),
        P(None, "mp", None),
        P(None, None, "mp"),
        P(None, "mp", None),
    )
    return jax.shard_map(
        shards, mesh=mesh, in_specs=placed, out_specs=P("dom", "mp"), check_vma=False
    )
```

```python
import functools

import jax
import jax.numpy as jnp
from jax import lax
from jax.experimental import pallas as pl
from jax.experimental.pallas import tpu as pltpu
from jax.sharding import PartitionSpec as P

HEAD_DIM = 64
BLK = 64
NBLK = 16
HB = 4
EPS = 1e-05
LOG2E = 1.4426950408889634
LEADS = (0, 1, 0, 1)
CUTS = ((1, 2, 4, 4), (4, 4, 4, 4))
F32 = jnp.float32
BF16 = jnp.bfloat16
MESH = pl.DeviceIdType.MESH


def normalize(values, gain_row):
    row_mean = jnp.mean(values, axis=-1, keepdims=True)
    centered = values - row_mean
    variance = jnp.mean(centered * centered, axis=-1, keepdims=True)
    return centered * lax.rsqrt(variance + EPS) * gain_row


def silu(v):
    return v / (1.0 + jnp.exp(-v))


def mm(a, b):
    return jnp.dot(a, b, preferred_element_type=F32)


def dot_nt(a, b):
    return lax.dot_general(a, b, (((1,), (1,)), ((), ())), preferred_element_type=F32)


def dot_tn(a, b):
    return lax.dot_general(a, b, (((0,), (0,)), ((), ())), preferred_element_type=F32)


def remote(src, dst, send, recv, where):
    return pltpu.make_async_remote_copy(
        src, dst, send, recv, device_id=where, device_id_type=MESH
    )


def mega(
    n_dom,
    n_mp,
    layers,
    nbr,
    feat_hbm,
    target_hbm,
    w1_hbm,
    b1_hbm,
    w2_hbm,
    egain_hbm,
    embed_hbm,
    bias_hbm,
    ln_hbm,
    qkv_hbm,
    out_hbm,
    up_hbm,
    down_hbm,
    result,
    feat,
    target,
    w1,
    b1,
    w2,
    egain,
    embed,
    bias_in,
    ln_gain,
    i_sem,
    bias,
    brecv,
    sbuf,
    sland,
    rbuf,
    rland,
    acc,
    psend,
    precv,
    xsend,
    xrecv,
    xown,
    nown,
    nhalo,
    kbuf,
    vbuf,
    qs,
    att,
    gq,
    gout,
    gup,
    gdown,
    fin,
    d_send,
    d_recv,
    b_send,
    b_recv,
    p_send,
    p_recv,
    x_send,
    x_recv,
    n_send,
    n_recv,
    c_send,
    c_recv,
    h_send,
    h_recv,
    r_send,
    r_recv,
    w_send,
    w_recv,
    f_send,
    f_recv,
    l_sem,
):
    dom = lax.axis_index("dom")
    m = lax.axis_index("mp")
    rows = feat.shape[0]
    cap = sbuf.shape[1]
    nodes, width = acc.shape
    cols = embed.shape[1]
    heads = cols // HEAD_DIM
    local_blocks = nodes // BLK
    per = local_blocks // n_mp
    edge = HB // n_mp
    span = per + 2 * edge
    prow = per // 2 * BLK
    core, side = m % 2, m // 2
    order_of = list(range(edge)) + list(range(per - edge, per)) + list(range(edge, per - edge))
    mine = (dom, m)
    peers = [(dom, m + 1 - 2 * (m % 2)), (dom, (m + 2) % 4), (dom, 3 - m)]
    beside = [((dom + n_dom - 1) % n_dom, m), ((dom + 1) % n_dom, m)]

    def across(n):
        e = 0
        bit = 1
        while bit < n_dom:
            own = (dom // bit) % 2
            e = e + ((1 - own) if n & bit else own) * bit
            bit *= 2
        return e

    barrier = pltpu.get_barrier_semaphore()
    for n in range(1, n_dom):
        pl.semaphore_signal(barrier, inc=1, device_id=(across(n), m), device_id_type=MESH)
    for p in peers:
        pl.semaphore_signal(barrier, inc=1, device_id=p, device_id_type=MESH)

    inputs = [
        pltpu.make_async_copy(src, dst, i_sem.at[j])
        for j, (src, dst) in enumerate(
            (
                (target_hbm, target),
                (feat_hbm, feat),
                (w1_hbm, w1),
                (b1_hbm, b1),
                (w2_hbm, w2),
                (egain_hbm, egain),
                (bias_hbm, bias_in),
                (embed_hbm, embed),
                (ln_hbm, ln_gain),
            )
        )
    ]
    for c in inputs:
        c.start()
    inputs[0].wait()

    owner = target[...] // nodes
    node = target[...] % nodes
    block = node // BLK
    held_by = block % n_mp
    nth = block // n_mp
    nth = jnp.where(
        nth < edge, nth, jnp.where(nth >= per - edge, nth - (per - 2 * edge), nth + edge)
    )
    place = (((held_by % 2) * 2 + held_by // 2) * per + nth) * BLK + node % BLK
    member = (lax.broadcasted_iota(jnp.int32, (n_dom, rows), 0) == owner).astype(F32)
    lanes = 128
    chunks = rows // lanes
    stacked = jnp.concatenate(
        [member[:, j * lanes : (j + 1) * lanes] for j in range(chunks)], axis=0
    ).astype(BF16)
    row_i = lax.broadcasted_iota(jnp.int32, (lanes, 2 * lanes), 0)
    col_i = lax.broadcasted_iota(jnp.int32, (lanes, 2 * lanes), 1)
    before = ((row_i < col_i) | (col_i >= lanes)).astype(F32).astype(BF16)
    counts = mm(stacked, before)
    running = jnp.zeros((n_dom, lanes), F32)
    ranks = []
    for j in range(chunks):
        part = counts[j * n_dom : (j + 1) * n_dom]
        here = (part[:, 0:lanes] + running) * member[:, j * lanes : (j + 1) * lanes]
        ranks.append(jnp.sum(here, axis=0, keepdims=True))
        running = running + part[:, lanes:]
    rank = jnp.concatenate(ranks, axis=1)
    hi = (place // 32).astype(F32)
    lo = (place % 32).astype(F32)
    pick = lax.broadcasted_iota(jnp.int32, (16, rows), 0)
    parts = jnp.where(
        pick == 0, hi, jnp.where(pick == 1, lo, jnp.where(pick == 2, 1.0, 0.0))
    ).astype(BF16)
    inputs[1].wait()
    features = feat[...]
    seat = lax.broadcasted_iota(jnp.int32, (cap, rows), 0).astype(F32).astype(BF16)

    def outgoing(n):
        wanted = jnp.where(owner == across(n), rank, -1.0).astype(BF16)
        here = jnp.where(seat == wanted, jnp.ones((), BF16), jnp.zeros((), BF16))
        sbuf[n] = mm(here, features).astype(BF16)
        where_to = dot_nt(parts, here)
        landed = where_to[0:1] * 32.0 + where_to[1:2]
        sland[n] = jnp.where(where_to[2:3] > 0.5, landed, -1.0).astype(jnp.int32)

    def d_copies(n):
        there = (across(n), m)
        return [
            remote(sbuf.at[n], rbuf.at[n], d_send.at[0, n], d_recv.at[0, n], there),
            remote(sland.at[n], rland.at[n], d_send.at[1, n], d_recv.at[1, n], there),
        ]

    def start_all(copies):
        for c in copies:
            c.start()

    sent = []

    def send(c):
        c.start()
        sent.append(c)
        return c

    arrays = ((qkv_hbm, gq), (out_hbm, gout), (up_hbm, gup), (down_hbm, gdown))
    bits = (dom % 2, (dom // 2) % 2)
    twins = ((dom + 1 - 2 * bits[0], m), (dom + 2 - 4 * bits[1], m))

    def part_of(ref, lead, i, h, cuts):
        size = ref.shape[-2] // cuts
        at = pl.ds(pl.multiple_of(h * size, size), size)
        return ref.at[lead + ((slice(None), at) if i == 0 else (at,))]

    def w_copy(k, l, i):
        own, got = arrays[i]
        first = LEADS[i]
        half = bits[1 - first]
        quarter = bits[first] + 2 * half
        cuts = CUTS[min(l, 1)][i]
        sems = (w_send.at[k, l, i], w_recv.at[k, l, i])
        if k == 0:
            h = (0, half, quarter)[cuts // 2]
            return remote(
                part_of(own, (l,), i, h, cuts), part_of(got, (l, 2), i, h, cuts), *sems, peers[1]
            )
        if k == 1:
            piece = part_of(got, (l, 2), i, quarter, 4)
            return remote(piece, piece, *sems, twins[first])
        if k == 2:
            return remote(own.at[l], got.at[l, 1], *sems, peers[0])
        if k == 5:
            piece = part_of(got, (l, 2), i, half, 2)
            return remote(piece, piece, *sems, twins[1 - first])
        if cuts == 1:
            return remote(got.at[l, 2], got.at[l, 3], *sems, peers[0])
        h = half if k == 3 else 1 - half
        return remote(part_of(got, (l, 2), i, h, 2), part_of(got, (l, 3), i, h, 2), *sems, peers[0])

    wc = {}

    def w_start(k, l, ids):
        if l < layers:
            for i in ids:
                wc[k, l, i] = send(w_copy(k, l, i))

    def w_next(k, l, ids):
        if l < layers:
            for i in ids:
                if (k, l, i) not in wc:
                    continue
                wc[k, l, i].wait_recv()
                after = {1: (5, 3), 5: (4,)}
                after[0] = {1: (3,), 2: (5, 3), 4: (1,)}[CUTS[min(l, 1)][i]]
                for j in after[k]:
                    w_start(j, l, (i,))

    def w_ready(l, ids, steps=(-1, 2, 3, 4)):
        for i in ids:
            for k in steps:
                if k < 0:
                    local[l, i].wait()
                elif (k, l, i) in wc:
                    wc[k, l, i].wait_recv()

    local = {
        (l, i): pltpu.make_async_copy(own.at[l], got.at[l, 0], l_sem.at[l, i])
        for l in range(layers)
        for i, (own, got) in enumerate(arrays)
    }

    far = list(range(n_dom - 1, 0, -1))
    outgoing(far[0])
    pl.semaphore_wait(barrier, n_dom - 1 + len(peers))
    w_start(0, 0, (0,))
    moving = {}
    for j, n in enumerate(far):
        if j:
            outgoing(n)
        moving[n] = d_copies(n)
        start_all(moving[n])
    w_start(0, 0, (1, 2, 3))
    for c in inputs[2:]:
        c.wait()
    for l in range(layers):
        w_start(2, l, (0, 1, 2, 3))
    for key in local:
        local[key].start()
    for o in range(n_mp):
        for r, i in enumerate(order_of):
            b = i * n_mp + o
            bias[o, r] = LOG2E * jnp.concatenate(
                [bias_in[h, :, b * BLK : (b + 1) * BLK] for h in range(heads)], axis=1
            )
    bc = [
        send(remote(bias.at[peers[k][1]], brecv.at[k], b_send.at[k], b_recv.at[k], peers[k]))
        for k in range(3)
    ]
    outgoing(0)

    def consume(buf, land, first):
        v = mm(buf, w1[...]) + b1[...]
        message = normalize(mm(silu(v).astype(BF16), w2[...]), egain[...]).astype(BF16)
        step = cap
        spot = lax.broadcasted_iota(jnp.int32, (step, cap), 0).astype(F32).astype(BF16)
        for c in range(nodes // step):
            goal = (land - c * step).astype(F32).astype(BF16)
            scatter = jnp.where(spot == goal, jnp.ones((), BF16), jnp.zeros((), BF16))
            at = slice(c * step, (c + 1) * step)
            if first:
                acc[at] = mm(scatter, message)
            else:
                acc[at] += mm(scatter, message)

    consume(sbuf[0], sland[0], True)
    my_cols = pl.ds(pl.multiple_of(m * cols, cols), cols)
    for o in range(n_mp):
        for r, i in enumerate(order_of):
            b = i * n_mp + o
            at = (((o % 2) * 2 + o // 2) * per + r) * BLK
            acc[at : at + BLK, my_cols] += embed[b * BLK : (b + 1) * BLK].astype(F32)
    w_start(0, 1, (0, 1, 2, 3))
    near = list(range(1, n_dom // 2))
    late = list(range(n_dom - 1, n_dom // 2 - 1, -1))
    for j, n in enumerate(near + late):
        for c in moving[n]:
            c.wait_recv()
        consume(rbuf[n], rland[n], False)
        if j == len(near) + len(late) // 2 - 1:
            w_next(0, 0, (0,))

    def acc_rows(c, rel, part):
        at = (c * 2 + (side + rel) % 2) * per * BLK + part * prow
        return pl.ds(pl.multiple_of(at, BLK), prow)

    pieces = [(0, 0), (1, 0), (0, 1), (1, 1)]
    pc = {}
    for rel, part in pieces:
        psend[rel, part] = acc[acc_rows(1 - core, rel, part), :].astype(BF16)
        pc[rel, part] = send(
            remote(psend.at[rel, part], precv.at[rel, part], p_send.at[rel, part], p_recv.at[rel, part], peers[0])
        )
    w_next(0, 0, (1, 2, 3))
    xc = {}
    for rel, part in pieces:
        pc[rel, part].wait_recv()
        xsend[rel, part] = (
            acc[acc_rows(core, rel, part), :] + precv[rel, part].astype(F32)
        ).astype(BF16)
        xc[rel, part] = send(
            remote(
                xsend.at[rel, part], xrecv.at[1 - rel, part], x_send.at[rel, part], x_recv.at[1 - rel, part], peers[1]
            )
        )

    def arrived(rel, part):
        remote(
            xsend.at[rel, part], xrecv.at[rel, part], x_send.at[rel, part], x_recv.at[rel, part], peers[1]
        ).wait_recv()

    w_next(0, 1, (0, 1, 2, 3))
    w_ready(0, (0,))
    for c in bc:
        c.wait_recv()

    ones = jnp.ones((NBLK * BLK, cols), BF16)
    lane = lax.broadcasted_iota(jnp.int32, (BLK, cols), 1) // HEAD_DIM
    block_count = local_blocks * n_dom

    def kv_index(b, t):
        away = nbr[b, t] - (dom * local_blocks - HB)
        away = jnp.where(away < 0, away + block_count, away)
        away = jnp.where(away >= block_count, away - block_count, away)
        away = jnp.minimum(away, local_blocks + 2 * HB - 1)
        o = away % n_mp
        role = ((o // 2 + side) % 2) * 2 + (o % 2 + core) % 2
        return role * span + away // n_mp

    cc, hc, rc, nc = {}, {}, {}, {}

    def spread(l, q, part):
        cc[q, part] = send(
            remote(
                nown.at[l, q, part], nown.at[l, q + 1, part], c_send.at[l, q // 2, part], c_recv.at[l, q // 2, part], peers[0]
            )
        )
        if part == 0:
            for s in range(2):
                hc[s, q] = send(
                    remote(
                        nown.at[l, q, 0, pl.ds(s * edge * BLK, edge * BLK)],
                        nhalo.at[l, 1 - s, q],
                        h_send.at[l, s, q // 2],
                        h_recv.at[l, 1 - s, q // 2],
                        beside[s],
                    )
                )

    def halo_arrived(l, s, q):
        remote(
            nhalo.at[l, s, q], nhalo.at[l, s, q], h_send.at[l, s, q // 2], h_recv.at[l, s, q // 2], beside[0]
        ).wait_recv()

    def relay_halo(l, s, q):
        rc[s, q] = send(
            remote(
                nhalo.at[l, s, q], nhalo.at[l, s, q + 1], r_send.at[l, s, q // 2], r_recv.at[l, s, q // 2], peers[0]
            )
        )

    def joined(l, c):
        return jnp.concatenate([gq[l, r, c] for r in range(n_mp)], axis=1)

    def project(l, found):
        x = jnp.concatenate([f[0] for f in found], axis=0)
        k = mm(x, joined(l, 1)).astype(BF16)
        v = mm(x, joined(l, 2)).astype(BF16)
        spots = [role * span + w for f in found for role, w in [(f[1], w) for w in f[2]]]
        for j, w in enumerate(spots):
            kbuf[w] = k[j * BLK : (j + 1) * BLK]
            vbuf[w] = v[j * BLK : (j + 1) * BLK]

    def own_part(l, role, part):
        n = per // 2
        return (nown[l, role, part], role, [edge + i for i in order_of[part * n : (part + 1) * n]])

    def halo_part(l, s, role):
        return (nhalo[l, s, role], role, [s * (span - edge) + i for i in range(edge)])

    def attend(l):
        for r, i in enumerate(order_of):
            b = i * n_mp + m
            index = [kv_index(b, t) for t in range(NBLK)]
            for p in range(n_mp):
                at = slice(p * cols, (p + 1) * cols)
                q = qs[r * BLK : (r + 1) * BLK, at]
                qbd = jnp.concatenate(
                    [jnp.where(lane == h, q.astype(F32), 0.0) for h in range(heads)], axis=0
                ).astype(BF16)
                keys = jnp.concatenate([kbuf[j, :, at] for j in index], axis=0)
                values = jnp.concatenate(
                    [jnp.concatenate([vbuf[j, :, at] for j in index], axis=0), ones], axis=1
                )
                lean = bias[m, r] if p == 0 else brecv[p - 1, r]
                s = dot_nt(keys, qbd).reshape(NBLK, BLK, heads * BLK) + lean[:, None, :]
                s = s.reshape(NBLK * BLK, heads * BLK)
                e = jnp.exp2(s - jnp.max(s, axis=0, keepdims=True)).astype(BF16)
                o = dot_tn(e, values)
                o = o[:, 0:cols] / o[:, cols : 2 * cols]
                merged = o[0:BLK]
                for h in range(1, heads):
                    merged = jnp.where(lane == h, o[h * BLK : (h + 1) * BLK], merged)
                att[r * BLK : (r + 1) * BLK, at] = merged.astype(BF16)

    for l in range(layers):
        gain = ln_gain[l, 0:1, :]
        if l == 0:
            def settle(rel, part):
                arrived(rel, part)
                x = (xsend[rel, part].astype(F32) + xrecv[rel, part].astype(F32)).astype(BF16)
                if rel == 0:
                    xown[part * prow : (part + 1) * prow] = x
                nown[0, 2 * rel, part] = normalize(x.astype(F32), gain).astype(BF16)
                spread(0, 2 * rel, part)

            settle(1, 0)
            settle(0, 0)
            project(l, [own_part(l, 0, 0), own_part(l, 2, 0)])
            settle(1, 1)
            w_next(1, 0, (1, 2, 3))
        else:
            for part in range(2):
                x = xown[part * prow : (part + 1) * prow].astype(F32)
                nown[l, 0, part] = normalize(x, gain).astype(BF16)
                nc[part] = send(
                    remote(
                        nown.at[l, 0, part], nown.at[l, 2, part], n_send.at[l, part], n_recv.at[l, part], peers[1]
                    )
                )
                spread(l, 0, part)
            w_next(5, l, (0,))
            w_ready(l, (0,))
            project(l, [own_part(l, 0, 0), own_part(l, 0, 1)])
            nc[0].wait_recv()
            spread(l, 2, 0)
        for q in (2, 0):
            cc[q, 0].wait_recv()
        if l == 0:
            project(l, [own_part(l, 1, 0), own_part(l, 3, 0)])
            settle(0, 1)
            project(l, [own_part(l, 0, 1), own_part(l, 2, 1)])
        else:
            project(l, [own_part(l, 2, 0), own_part(l, 1, 0), own_part(l, 3, 0)])
            nc[1].wait_recv()
            spread(l, 2, 1)
        x = jnp.concatenate([nown[l, 0, 0], nown[l, 0, 1]], axis=0)
        qs[...] = (mm(x, joined(l, 0)) * (HEAD_DIM ** (-0.5) * LOG2E)).astype(BF16)
        for q in (0, 2):
            for s in range(2):
                halo_arrived(l, s, q)
                relay_halo(l, s, q)
        w_next(5, l, (1,))
        for q in (0, 2):
            cc[q, 1].wait_recv()
        if l == 0:
            rest = [own_part(l, 1, 1), own_part(l, 3, 1)]
        else:
            rest = [own_part(l, 2, 1), own_part(l, 1, 1), own_part(l, 3, 1)]
        project(l, rest + [halo_part(l, s, q) for q in (0, 2) for s in range(2)])
        for key in rc:
            rc[key].wait_recv()
        project(l, [halo_part(l, s, q + 1) for q in (0, 2) for s in range(2)])
        if l == 0:
            w_next(1, 1, (0, 1, 2, 3))
        attend(l)
        w_next(5, l, (2, 3))
        w_ready(l, (1,))
        mixed = jnp.concatenate([gout[l, r] for r in range(n_mp)], axis=0)
        x1 = (xown[...].astype(F32) + mm(att[...], mixed)).astype(BF16).astype(F32)
        n2 = normalize(x1, ln_gain[l, 1:2, :]).astype(BF16)
        total = x1
        for r in range(n_mp):
            w_ready(l, (2, 3), ((-1,), (2,), (), (3, 4))[r])
            total = total + mm(silu(mm(n2, gup[l, r])).astype(BF16), gdown[l, r])
        if l + 1 < layers:
            xown[...] = total.astype(BF16)
        else:
            for r, i in enumerate(order_of):
                fin[i] = total[r * BLK : (r + 1) * BLK].astype(BF16)

    fc = []
    for k in (1, 2, 0):
        there = peers[k][1]
        fc.append(
            send(
                remote(
                    fin.at[:, :, pl.ds(pl.multiple_of(there * cols, cols), cols)],
                    result.at[:, m],
                    f_send.at[k],
                    f_recv.at[k],
                    peers[k],
                )
            )
        )
    result[:, m] = fin[:, :, my_cols]
    for n in far:
        for c in moving[n]:
            c.wait_send()
    for c in sent:
        c.wait_send()
    for c in fc:
        c.wait_recv()


def shards(
    grid_feat,
    grid_target,
    enc_w1,
    enc_b1,
    enc_w2,
    enc_gain,
    mesh_embed,
    nbr_blocks,
    attn_bias,
    ln_gain,
    qkv_w,
    out_w,
    up_w,
    down_w,
):
    n_dom = lax.axis_size("dom")
    n_mp = lax.axis_size("mp")
    rows, f_in = grid_feat.shape
    width = enc_w2.shape[1]
    cols = width // n_mp
    nodes = mesh_embed.shape[0]
    heads = cols // HEAD_DIM
    layers = ln_gain.shape[0]
    cap = 2 * rows // n_dom
    per = nodes // BLK // n_mp
    edge = HB // n_mp
    prow = per // 2 * BLK
    ff = up_w.shape[2]
    vmem = pl.BlockSpec(memory_space=pltpu.VMEM)
    dma = pltpu.SemaphoreType.DMA
    out = pl.pallas_call(
        functools.partial(mega, n_dom, n_mp, layers),
        out_shape=jax.ShapeDtypeStruct((per, n_mp, BLK, cols), BF16),
        in_specs=[pl.BlockSpec(memory_space=pltpu.SMEM)] + [pl.BlockSpec(memory_space=pl.ANY)] * 13,
        out_specs=vmem,
        scratch_shapes=[
            pltpu.VMEM(grid_feat.shape, BF16),
            pltpu.VMEM((1, rows), jnp.int32),
            pltpu.VMEM(enc_w1.shape, BF16),
            pltpu.VMEM((1, width), F32),
            pltpu.VMEM(enc_w2.shape, BF16),
            pltpu.VMEM((1, width), F32),
            pltpu.VMEM(mesh_embed.shape, BF16),
            pltpu.VMEM(attn_bias.shape, F32),
            pltpu.VMEM(ln_gain.shape, F32),
            dma((9,)),
            pltpu.VMEM((n_mp, per, NBLK, heads * BLK), F32),
            pltpu.VMEM((3, per, NBLK, heads * BLK), F32),
            pltpu.VMEM((n_dom, cap, f_in), BF16),
            pltpu.VMEM((n_dom, 1, cap), jnp.int32),
            pltpu.VMEM((n_dom, cap, f_in), BF16),
            pltpu.VMEM((n_dom, 1, cap), jnp.int32),
            pltpu.VMEM((nodes, width), F32),
            pltpu.VMEM((2, 2, prow, width), BF16),
            pltpu.VMEM((2, 2, prow, width), BF16),
            pltpu.VMEM((2, 2, prow, width), BF16),
            pltpu.VMEM((2, 2, prow, width), BF16),
            pltpu.VMEM((per * BLK, width), BF16),
            pltpu.VMEM((layers, n_mp, 2, prow, width), BF16),
            pltpu.VMEM((layers, 2, n_mp, edge * BLK, width), BF16),
            pltpu.VMEM((n_mp * (per + 2 * edge), BLK, width), BF16),
            pltpu.VMEM((n_mp * (per + 2 * edge), BLK, width), BF16),
            pltpu.VMEM((per * BLK, width), BF16),
            pltpu.VMEM((per * BLK, width), BF16),
            pltpu.VMEM((layers, n_mp) + qkv_w.shape[1:], BF16),
            pltpu.VMEM((layers, n_mp) + out_w.shape[1:], BF16),
            pltpu.VMEM((layers, n_mp, width, ff), BF16),
            pltpu.VMEM((layers, n_mp, ff, width), BF16),
            pltpu.VMEM((per, BLK, width), BF16),
            dma((2, n_dom)),
            dma((2, n_dom)),
            dma((3,)),
            dma((3,)),
            dma((2, 2)),
            dma((2, 2)),
            dma((2, 2)),
            dma((2, 2)),
            dma((layers, 2)),
            dma((layers, 2)),
            dma((layers, 2, 2)),
            dma((layers, 2, 2)),
            dma((layers, 2, 2)),
            dma((layers, 2, 2)),
            dma((layers, 2, 2)),
            dma((layers, 2, 2)),
            dma((6, layers, 4)),
            dma((6, layers, 4)),
            dma((3,)),
            dma((3,)),
            dma((layers, 4)),
        ],
        compiler_params=pltpu.CompilerParams(
            collective_id=0, has_side_effects=True, vmem_limit_bytes=60 * 1024 * 1024
        ),
    )(
        nbr_blocks,
        grid_feat,
        grid_target.reshape(1, rows),
        enc_w1,
        enc_b1.reshape(1, width),
        enc_w2,
        enc_gain.reshape(1, width),
        mesh_embed,
        attn_bias,
        ln_gain,
        qkv_w,
        out_w,
        up_w,
        down_w,
    )
    return out.reshape(nodes, cols)


def solution(mesh):
    placed = (
        P(("dom", "mp"), None),
        P(("dom", "mp")),
        P(),
        P(),
        P(),
        P(),
        P("dom", "mp"),
        P("dom", None),
        P("mp", None, "dom"),
        P(),
        P(None, None, None, "mp"),
        P(None, "mp", None),
        P(None, None, "mp"),
        P(None, "mp", None),
    )
    return jax.shard_map(
        shards, mesh=mesh, in_specs=placed, out_specs=P("dom", "mp"), check_vma=False
    )
```
